512 devices in a mesh: seq: 64 (over y, z), mp: 8 (over x, core).
Axes of the slice: x: 4, y: 4, z: 16, core: 2. Of those that a mesh axis runs over, the one named last changes fastest.
Arguments:
- byte_states: bfloat16 [16384, 1024], P('seq'), may hold values from -6 to 6
- outer_gain: float32 [1024], replicated, may hold values from 0.1 to 1.9
- mamba_input: bfloat16 [1024, 1024], P(None, 'mp'), may hold values from -0.1875 to 0.1875
- mamba_step: bfloat16 [1024, 1024], P(None, 'mp'), may hold values from -0.1875 to 0.1875
- decay_rate: float32 [1024], P('mp'), as said below
- mixer_weight: bfloat16 [1024, 1024], P('mp'), may hold values from -0.1875 to 0.1875
- boundaries: int32 [64, 128], P('seq'), may hold values from 0 to 256, as said below
- span_counts: int32 [64], replicated, may hold values from 1 to 128, as said below
- up_weight: bfloat16 [1024, 4096], P('seq', 'mp'), may hold values from -0.1875 to 0.1875
- up_bias: float32 [4096], P('mp'), may hold values from -5 to 5
- inner_gain: float32 [4096], replicated, as said below
- query_weight: bfloat16 [4096, 4096], P('seq', 'mp'), as said below
- key_weight: bfloat16 [4096, 1024], P('seq', 'mp'), as said below
- value_weight: bfloat16 [4096, 1024], P('seq', 'mp'), may hold values from -0.09375 to 0.09375
- return_weight: bfloat16 [4096, 1024], P('mp'), may hold values from -0.09375 to 0.09375
Outputs:
- joined: bfloat16 [16384, 1024], P('seq', 'mp')
The draws below stay inside these ranges and needn't reach their ends.
Inputs may be any that keep to these rules, and one draw needn't show every extreme that they name: `boundaries`: row s lists the spans of shard s: its first span_counts[s] entries rise strictly from 0 and are byte positions within the shard; each span runs to the next entry, the last to the shard's end; the other entries equal 256. `span_counts`: the counts sum to 4096; some shard has exactly 128 spans. `decay_rate`: Positive. `inner_gain`: Positive. `query_weight`: Finite. `key_weight`: Finite.
All inputs are finite; a program needn't handle non-finite values.
Results may differ from the reference program's by a relative error of at most 0.01.
Values may be sent and summed in bfloat16 or wider, within the bound.
A program may use at most 64 MiB of HBM per device.

```python
import math
import jax
import jax.numpy as jnp
from jax import lax

DO = 1024
DI = 4096
HEADS = 32
KV_HEADS = 8
HEAD = 128
ROWS = 256
CAP = 128
TOTAL = 4096
BYTES = 16384
N_SEQ = 64


def span_plan(key):
    plan_key = jax.random.fold_in(key, 71)
    special = jax.random.randint(jax.random.fold_in(plan_key, 1), (), 0, N_SEQ)
    weights = jax.random.randint(jax.random.fold_in(plan_key, 2), (N_SEQ,), 8, 17)
    shard_ids = jnp.arange(N_SEQ, dtype=jnp.int32)
    others = shard_ids != special
    weights = jnp.where(others, weights, 0)
    spare_rows = TOTAL - CAP - (N_SEQ - 1)
    shares = spare_rows * weights // jnp.sum(weights)
    leftover = spare_rows - jnp.sum(shares)
    other_rank = jnp.cumsum(others.astype(jnp.int32)) - 1
    extra_one = (others & (other_rank < leftover)).astype(jnp.int32)
    counts = jnp.where(others, 1 + shares + extra_one, CAP).astype(jnp.int32)

    def one_shard(shard_number, span_total):
        shuffled = jax.random.permutation(jax.random.fold_in(plan_key, 100 + shard_number), ROWS - 1)
        chosen = jnp.concatenate([jnp.ones((1,), bool), shuffled < span_total - 1])
        positions = jnp.where(chosen, jnp.arange(ROWS, dtype=jnp.int32), ROWS)
        return jnp.sort(positions)[:CAP].astype(jnp.int32)
    marks = jax.vmap(one_shard)(shard_ids, counts)
    return (counts, marks)


def draw_boundaries(key, part):
    return span_plan(key)[1]


def draw_span_counts(key, part):
    return span_plan(key)[0]


def draw_decay_rate(key, part):
    choose_slow = jax.random.randint(jax.random.fold_in(key, 3), (DO,), 0, 10)
    slow_mask = choose_slow < 5
    uniform_draw = jax.random.uniform(jax.random.fold_in(key, 4), (DO,), jnp.float32)
    slow_rate = jnp.exp(jnp.log(0.1 / BYTES) + uniform_draw * jnp.log(20.0))
    fast_rate = jnp.exp(jnp.log(1.0 / 50.0) + uniform_draw * jnp.log(50.0 / 30.0))
    return jnp.where(slow_mask, slow_rate, fast_rate).astype(jnp.float32)


def draw_inner_gain(key, part):
    uniform_draw = jax.random.uniform(jax.random.fold_in(key, 5), (DI,), jnp.float32)
    return (0.7 + 0.6 * uniform_draw).astype(jnp.float32)


def draw_up_bias(key, part):
    uniform_draw = jax.random.uniform(jax.random.fold_in(key, 21), (DI,), jnp.float32)
    return (2.0 * uniform_draw - 1.0).astype(jnp.float32)


def projection_base(key):
    return jax.random.truncated_normal(jax.random.fold_in(key, 31), -4.0, 4.0, (DI, KV_HEADS * HEAD), jnp.float32)


def draw_key_weight(key, part):
    return (projection_base(key) / math.sqrt(DI)).astype(jnp.bfloat16)


def draw_query_weight(key, part):
    noise = jax.random.truncated_normal(jax.random.fold_in(key, 32), -4.0, 4.0, (DI, HEADS * HEAD), jnp.float32)
    return (3.0 * noise / math.sqrt(DI)).astype(jnp.bfloat16)


def steps_of(stream_key, dims, cuts, least, largest):
    loudness, own = 1.0, jax.random.fold_in(stream_key, 6)
    for dim, shards_of in cuts:
        draws = jnp.exp(jax.random.uniform(jax.random.fold_in(own, dim), (shards_of,), jnp.float32, least / len(cuts), largest / len(cuts)))
        loudness = loudness * jnp.repeat(draws, dims[dim] // shards_of).reshape([-1 if axis == dim else 1 for axis in range(len(dims))])
    return loudness


def gaussian(key, dims, scale, most, shards=(), held_as=jnp.bfloat16):
    values = jax.random.normal(key, dims, jnp.float32) * scale
    if len(shards) > 0:
        values = steps_of(key, dims, shards, -0.22, 0.18) * values
    return jnp.clip(values, min=-most, max=most).astype(held_as)


def setup_inputs(seed: int = 0) -> dict:
    key_list = jax.random.split(jax.random.key(seed), 16)
    return {
        "byte_states": gaussian(key_list[0], (BYTES, DO), 1.0, 6.0, ((0, 64),)),
        "outer_gain": jnp.clip(1.0 + 0.18 * jax.random.normal(key_list[1], (DO,), jnp.float32), 0.1, 1.9),
        "mamba_input": gaussian(key_list[2], (DO, DO), DO ** -0.5, 0.1875, ((1, 8),)),
        "mamba_step": gaussian(key_list[3], (DO, DO), DO ** -0.5, 0.1875, ((1, 8),)),
        "decay_rate": draw_decay_rate(jax.random.fold_in(key_list[15], 71), 0),
        "mixer_weight": gaussian(key_list[5], (DO, DO), DO ** -0.5, 0.1875, ((0, 8),)),
        "boundaries": draw_boundaries(jax.random.fold_in(key_list[15], 71), 0),
        "span_counts": draw_span_counts(jax.random.fold_in(key_list[15], 71), 0),
        "up_weight": gaussian(key_list[8], (DO, DI), DO ** -0.5, 0.1875, ((0, 64), (1, 8))),
        "up_bias": draw_up_bias(jax.random.fold_in(key_list[15], 71), 0),
        "inner_gain": draw_inner_gain(jax.random.fold_in(key_list[15], 71), 0),
        "query_weight": draw_query_weight(jax.random.fold_in(key_list[15], 71), 0),
        "key_weight": draw_key_weight(jax.random.fold_in(key_list[15], 71), 0),
        "value_weight": gaussian(key_list[13], (DI, KV_HEADS * HEAD), DI ** -0.5, 0.09375, ((0, 64), (1, 8))),
        "return_weight": gaussian(key_list[14], (HEADS * HEAD, DO), (HEADS * HEAD) ** -0.5, 0.09375, ((0, 8),)),
    }


eps = 1e-05
masked = -1e+30

def rms_scale(values, gain):
    values = values.astype(jnp.float32)
    return values * lax.rsqrt(lax.optimization_barrier(jnp.mean(values * values, axis=-1, keepdims=True)) + eps) * gain

def advance(carried, factors):
    carried = factors[0] * carried + factors[1]
    return (carried, carried)

def reference(byte_states, outer_gain, mamba_input, mamba_step, decay_rate, mixer_weight, boundaries, span_counts, up_weight, up_bias, inner_gain, query_weight, key_weight, value_weight, return_weight):
    normed = rms_scale(byte_states, outer_gain).astype(jnp.bfloat16)
    inputs = jnp.dot(normed, mamba_input, preferred_element_type=jnp.float32)
    step_sizes = jax.nn.softplus(jnp.dot(normed, mamba_step, preferred_element_type=jnp.float32))
    rate_steps = step_sizes * decay_rate
    decays = jnp.exp(-rate_steps)
    drives = jnp.sqrt(-jnp.expm1(-2.0 * rate_steps)) * inputs
    _, states = lax.scan(advance, jnp.zeros((DO,), jnp.float32), (decays, drives))
    mixed_sum = jnp.dot(states.astype(jnp.bfloat16), mixer_weight, preferred_element_type=jnp.float32)
    encoded = (byte_states.astype(jnp.float32) + mixed_sum).astype(jnp.bfloat16)
    counts = span_counts.astype(jnp.int32)
    offsets = (jnp.cumsum(counts) - counts).astype(jnp.int32)
    slot_ids = jnp.arange(CAP, dtype=jnp.int32)
    live_slots = slot_ids[None, :] < counts[:, None]
    target = jnp.where(live_slots, offsets[:, None] + slot_ids[None, :], TOTAL).reshape(-1).astype(jnp.int32)
    shard_ids = jnp.arange(N_SEQ, dtype=jnp.int32)
    source_row = (shard_ids[:, None] * ROWS + jnp.minimum(boundaries, ROWS - 1)).reshape(-1).astype(jnp.int32)
    picked = jnp.zeros((TOTAL,), jnp.int32).at[target].set(source_row, mode='drop')
    pooled = encoded[picked]
    widened = (jnp.dot(pooled, up_weight, preferred_element_type=jnp.float32) + up_bias[None, :]).astype(jnp.bfloat16)
    inner_normed = rms_scale(widened, inner_gain).astype(jnp.bfloat16)
    queries = jnp.dot(inner_normed, query_weight, preferred_element_type=jnp.float32).astype(jnp.bfloat16)
    key_rows = jnp.dot(inner_normed, key_weight, preferred_element_type=jnp.float32).astype(jnp.bfloat16)
    value_rows = jnp.dot(inner_normed, value_weight, preferred_element_type=jnp.float32).astype(jnp.bfloat16)
    span_order = jnp.arange(TOTAL, dtype=jnp.int32)
    allowed = span_order[None, :] <= span_order[:, None]
    group_size = HEADS // KV_HEADS
    score_scale = 1.0 / math.sqrt(HEAD)

    def one_head(head_number):
        head_query = lax.dynamic_slice_in_dim(queries, head_number * HEAD, HEAD, 1)
        shared = head_number // group_size
        head_key = lax.dynamic_slice_in_dim(key_rows, shared * HEAD, HEAD, 1)
        head_value = lax.dynamic_slice_in_dim(value_rows, shared * HEAD, HEAD, 1)
        scores = jnp.dot(head_query, head_key.T, preferred_element_type=jnp.float32) * score_scale
        scores = jnp.where(allowed, scores, masked)
        row_peak = lax.optimization_barrier(jnp.max(scores, axis=1, keepdims=True))
        lifted = jnp.exp(scores - row_peak)
        denominator = lax.optimization_barrier(jnp.sum(lifted, axis=1, keepdims=True))
        weighted = jnp.dot(lifted.astype(jnp.bfloat16), head_value, preferred_element_type=jnp.float32)
        return (weighted / denominator).astype(jnp.bfloat16)
    per_head = lax.map(one_head, jnp.arange(HEADS, dtype=jnp.int32))
    attended = jnp.transpose(per_head, (1, 0, 2)).reshape(TOTAL, HEADS * HEAD)
    returned = jnp.dot(attended, return_weight, preferred_element_type=jnp.float32).astype(jnp.bfloat16)
    positions = jnp.arange(ROWS, dtype=jnp.int32)
    passed = lax.optimization_barrier(jnp.sum(((boundaries[:, None, :] <= positions[None, :, None]) & live_slots[:, None, :]).astype(jnp.int32), axis=2))
    span_ids = (offsets[:, None] + passed - 1).reshape(-1).astype(jnp.int32)
    return (encoded.astype(jnp.float32) + returned[span_ids].astype(jnp.float32)).astype(jnp.bfloat16)
```

```python
import math

import jax
import jax.numpy as jnp
from jax import lax
from jax.experimental import pallas as pl
from jax.experimental.pallas import tpu as pltpu
from jax.sharding import PartitionSpec as P

HEADS = 32
KV_HEADS = 8
HEAD = 128
NY, NZ = 4, 16
NX, NC = 4, 2
CAP = 128
KV_A = 48

eps = 1e-05
masked = -1e30
far_index = 1073741824

MESH = pl.DeviceIdType.MESH
VM = pl.BlockSpec(memory_space=pltpu.VMEM)
DMA = pltpu.SemaphoreType.DMA


def coords():
    s, m = lax.axis_index("seq"), lax.axis_index("mp")
    return s // NZ, s % NZ, m // NC, m % NC


def remote(src, dst, ss, rs, y, z, m):
    return pltpu.make_async_remote_copy(
        src_ref=src, dst_ref=dst, send_sem=ss, recv_sem=rs, device_id=(y * NZ + z, m), device_id_type=MESH
    )


def enter(peers):
    barrier = pltpu.get_barrier_semaphore()
    for seq, mp in peers:
        pl.semaphore_signal(barrier, inc=1, device_id=(seq, mp), device_id_type=MESH)
    pl.semaphore_wait(barrier, len(peers))


def yz_peers(y, z, m):
    return [
        (y * NZ + (z + 1) % NZ, m),
        (y * NZ + (z + NZ - 1) % NZ, m),
        ((y + 1) % NY * NZ + z, m),
        ((y + NY - 1) % NY * NZ + z, m),
    ]


def mp_peers(s, x, c):
    same = [(s, ((x + k) % NX) * NC + c) for k in range(1, NX)]
    return same + [(s, x * NC + 1 - c)]


class RingY:
    def __init__(self, buf, ss, rs, cut, place):
        self.buf, self.ss, self.rs, self.cut = buf, ss, rs, cut
        self.y, self.z, self.m = place

    def part(self, yy, zz, k):
        ref = self.buf.at[yy % NY, zz]
        rows = self.buf.shape[2]
        if k == 2:
            return ref.at[pl.ds(0, self.cut)]
        if k == 3:
            return ref.at[pl.ds(self.cut, rows - self.cut)]
        return ref

    def copy(self, k, yy, zz, src=None):
        up = k in (0, 2)
        ref = self.part(yy, zz, k)
        return remote(
            ref if src is None else src,
            ref,
            self.ss.at[k, zz],
            self.rs.at[k, zz],
            (self.y + (1 if up else NY - 1)) % NY,
            self.z,
            self.m,
        )

    def start(self, zz, src=None):
        self.copy(0, self.y, zz, src).start()
        self.copy(1, self.y, zz, src).start()

    def relay(self, zz):
        self.copy(0, self.y + NY - 1, zz).wait_recv()
        self.copy(2, self.y + NY - 1, zz).start()
        self.copy(1, self.y + 1, zz).wait_recv()
        self.copy(3, self.y + 1, zz).start()

    def finish(self, zz):
        self.copy(2, self.y + 2, zz).wait_recv()
        self.copy(3, self.y + 2, zz).wait_recv()

    def drain(self, zz):
        for k, yy in ((0, self.y), (1, self.y), (2, self.y + NY - 1), (3, self.y + 1)):
            self.copy(k, yy, zz).wait_send()


class RingZ:
    def __init__(self, view, ss, rs, place):
        self.view, self.ss, self.rs = view, ss, rs
        self.y, self.z, self.m = place

    def item(self, d, t):
        return (self.z + (NZ - t if d == 0 else t)) % NZ

    def copy(self, d, t, zz, src=None):
        ref = self.view(zz)
        return remote(
            ref if src is None else src,
            ref,
            self.ss.at[d, t],
            self.rs.at[d, t],
            self.y,
            (self.z + (1 if d == 0 else NZ - 1)) % NZ,
            self.m,
        )

    def send(self, d, t, src=None):
        self.copy(d, t, self.item(d, t), src).start()

    def arrive(self, d, t):
        self.copy(d, t - 1, self.item(d, t)).wait_recv()

    def drain(self, d, t):
        self.copy(d, t, self.item(d, t)).wait_send()


STEPS = (8, 7)


def gather_two(yf, yf_own, zf, zf_own, y, z, m, cut_yf, cut_zf, sems):
    yss, yrs, zss, zrs, yss2, yrs2, zss2, zrs2, lsem = sems
    place = (y, z, m)
    a_y = RingY(yf, yss, yrs, cut_yf, place)
    a_z = RingZ(lambda zz: yf.at[:, zz], zss, zrs, place)
    b_y = RingY(zf, yss2, yrs2, cut_zf, place)
    b_z = RingZ(lambda zz: zf.at[y, zz], zss2, zrs2, place)
    locals_ = [
        pltpu.make_async_copy(src, dst, lsem.at[i])
        for i, (src, dst) in enumerate(
            [(src, yf.at[y, z].at[:, cols]) for src, cols in yf_own] + [(zf_own, zf.at[y, z])]
        )
    ]
    for cp in locals_:
        cp.start()
    for cp in locals_:
        cp.wait()
    a_y.start(z)
    b_z.send(0, 0)
    b_z.send(1, 0)
    b_y.start(z)
    a_y.relay(z)
    a_y.finish(z)
    a_z.send(0, 0)
    a_z.send(1, 0)
    b_y.relay(z)

    def step(t, _):
        for d in range(2):
            @pl.when(t <= STEPS[d])
            def _():
                b_z.arrive(d, t)

                @pl.when(t < STEPS[d])
                def _():
                    b_z.send(d, t)

                b_y.start(b_z.item(d, t))
        for d in range(2):
            @pl.when(t <= STEPS[d])
            def _():
                a_z.arrive(d, t)

                @pl.when(t < STEPS[d])
                def _():
                    a_z.send(d, t)
        for d in range(2):
            @pl.when(t <= STEPS[d])
            def _():
                b_y.relay(b_z.item(d, t))
        return 0

    lax.fori_loop(1, 9, step, 0)

    def close(zz, _):
        b_y.finish(zz)
        b_y.drain(zz)
        return 0

    lax.fori_loop(0, NZ, close, 0)
    a_y.drain(z)

    def close_z(t, _):
        for ring in (a_z, b_z):
            for d in range(2):
                @pl.when(t < STEPS[d])
                def _():
                    ring.drain(d, t)
        return 0

    lax.fori_loop(0, 8, close_z, 0)


def gather_sems(n_local):
    return [
        DMA((4, NZ)), DMA((4, NZ)), DMA((2, 8)), DMA((2, 8)),
        DMA((4, NZ)), DMA((4, NZ)), DMA((2, 8)), DMA((2, 8)),
        DMA((n_local,)),
    ]


class MpGather:
    def __init__(self, view, ss, rs, place):
        self.view, self.ss, self.rs = view, ss, rs
        self.s, self.x, self.c = place

    def push(self, k, src=None):
        mine = self.x * NC + self.c
        ref = self.view(mine)
        return pltpu.make_async_remote_copy(
            src_ref=ref if src is None else src, dst_ref=ref, send_sem=self.ss.at[k], recv_sem=self.rs.at[k],
            device_id=(self.s, ((self.x + k) % NX) * NC + self.c), device_id_type=MESH,
        )

    def came(self, k):
        ref = self.view(((self.x + NX - k) % NX) * NC + self.c)
        return pltpu.make_async_remote_copy(
            src_ref=ref, dst_ref=ref, send_sem=self.ss.at[k], recv_sem=self.rs.at[k],
            device_id=(self.s, ((self.x + k) % NX) * NC + self.c), device_id_type=MESH,
        )

    def across(self, k, core):
        ref = self.view(((self.x + NX - k) % NX) * NC + core)
        return pltpu.make_async_remote_copy(
            src_ref=ref, dst_ref=ref, send_sem=self.ss.at[4 + k], recv_sem=self.rs.at[4 + k],
            device_id=(self.s, self.x * NC + 1 - self.c), device_id_type=MESH,
        )

    def start(self):
        for k in (2, 1, 3):
            self.push(k).start()
        self.across(0, self.c).start()

    def relay(self):
        for k in (1, 3, 2):
            self.came(k).wait_recv()
            self.across(k, self.c).start()

    def finish(self):
        for k in (0, 1, 3, 2):
            self.across(k, 1 - self.c).wait_recv()

    def drain(self):
        for k in (1, 2, 3):
            self.push(k).wait_send()
        for k in range(4):
            self.across(k, self.c).wait_send()


def weights_kernel(u_ref, q_ref, k_ref, v_ref, u_out, kv_out, q_out, us, uy, kss, krs, *sems):
    y, z, x, c = coords()
    m = x * NC + c
    enter(yz_peers(y, z, m))
    place = (y, z, m)
    u_y = RingY(u_out, us.at[0], us.at[1], 8, place)
    u_z = RingZ(lambda zz: u_out.at[:, zz], kss, krs, place)
    cp = pltpu.make_async_copy(u_ref, u_out.at[y, z], uy.at[0])
    cp.start()
    cp.wait()
    u_y.start(z)
    u_y.relay(z)
    u_y.finish(z)
    u_z.send(0, 0)
    u_z.send(1, 0)
    gather_two(
        kv_out, [(k_ref, pl.ds(0, HEAD)), (v_ref, pl.ds(HEAD, HEAD))], q_out, q_ref, y, z, m, 32, 32, sems
    )

    def step(t, _):
        for d in range(2):
            @pl.when(t <= STEPS[d])
            def _():
                u_z.arrive(d, t)

                @pl.when(t < STEPS[d])
                def _():
                    u_z.send(d, t)
        return 0

    lax.fori_loop(1, 9, step, 0)
    u_y.drain(z)

    def close_z(t, _):
        for d in range(2):
            @pl.when(t < STEPS[d])
            def _():
                u_z.drain(d, t)
        return 0

    lax.fori_loop(0, 8, close_z, 0)


def params(cid, mib=56):
    return pltpu.CompilerParams(collective_id=cid, has_side_effects=True, vmem_limit_bytes=mib << 20)


def gather_weights(up_weight, query_weight, key_weight, value_weight):
    bf = jnp.bfloat16
    u, kv, q = pl.pallas_call(
        weights_kernel,
        out_shape=[
            jax.ShapeDtypeStruct((NY, NZ, 16, 512), bf),
            jax.ShapeDtypeStruct((NY, NZ, 64, 256), bf),
            jax.ShapeDtypeStruct((NY, NZ, 64, 512), bf),
        ],
        in_specs=[VM] * 4,
        out_specs=[VM] * 3,
        scratch_shapes=[DMA((2, 4, NZ)), DMA((1,)), DMA((2, 8)), DMA((2, 8))] + gather_sems(3),
        compiler_params=params(1),
        name="weights",
    )(up_weight, query_weight, key_weight, value_weight)
    return u.reshape(1024, 512), kv.reshape(4096, 256), q.reshape(4096, 512)


def one_minus_exp(v):
    series = v * (1.0 - v * (0.5 - v * (1 / 6 - v * (1 / 24 - v * (1 / 120 - v / 720)))))
    return jnp.where(v < 0.25, series, 1.0 - jnp.exp(-v))


def scan_rows(decays, drives):
    rows = decays.shape[0]
    ids = lax.broadcasted_iota(jnp.int32, decays.shape, 0)
    k = 1
    while k < rows:
        if k < 8:
            a_back = jnp.where(ids >= k, pltpu.roll(decays, k, 0), 1.0)
            b_back = jnp.where(ids >= k, pltpu.roll(drives, k, 0), 0.0)
        else:
            a_back = jnp.concatenate([jnp.ones((k, decays.shape[1]), jnp.float32), decays[: rows - k]], 0)
            b_back = jnp.concatenate([jnp.zeros((k, decays.shape[1]), jnp.float32), drives[: rows - k]], 0)
        drives = decays * b_back + drives
        decays = decays * a_back
        k *= 2
    return decays, drives


def scan_kernel(
    bytes_ref, gain_ref, win_ref, wstep_ref, rate_ref, mixer_ref,
    states_ref, mixfull_ref,
    pair_ref, line_ref, total_ref, col_ref, pzs, pzr, pys, pyr, gs, gr, ms, mr, lsem,
):
    y, z, x, c = coords()
    s, m = y * NZ + z, x * NC + c
    peers = [(y * NZ + (z + k) % NZ, m) for k in range(1, NZ)]
    peers += [((y + k) % NY * NZ + z, m) for k in range(1, NY)]
    enter(peers + mp_peers(s, x, c))
    mixer = MpGather(lambda mm: mixfull_ref.at[pl.ds(pl.multiple_of(mm * 128, 128), 128)], ms, mr, (s, x, c))
    cp = pltpu.make_async_copy(mixer_ref, mixer.view(m), lsem.at[0])
    cp.start()
    cp.wait()
    mixer.start()

    values = bytes_ref[...].astype(jnp.float32)
    scale = lax.rsqrt(jnp.mean(values * values, axis=-1, keepdims=True) + eps)
    normed = (values * scale * gain_ref[...]).astype(jnp.bfloat16)
    inputs = jnp.dot(normed, win_ref[...], preferred_element_type=jnp.float32)
    raw = jnp.dot(normed, wstep_ref[...], preferred_element_type=jnp.float32)
    small = jnp.exp(-jnp.abs(raw))
    rate = (jnp.maximum(raw, 0.0) + jnp.log1p(small)) * rate_ref[...]
    decays = jnp.exp(-rate)
    drives = jnp.sqrt(one_minus_exp(2.0 * rate)) * inputs
    through, local = scan_rows(decays, drives)
    tile = jnp.concatenate([through[255:256], local[255:256], jnp.zeros((6, 128), jnp.float32)], 0)
    pair_ref[...] = tile
    line_ref[z] = tile

    def zpush(k):
        return remote(pair_ref, line_ref.at[z], pzs.at[k], pzr.at[k], y, (z + k) % NZ, m)

    def zcame(k):
        zz = (z + NZ - k) % NZ
        return remote(pair_ref, line_ref.at[zz], pzs.at[k], pzr.at[k], y, (z + k) % NZ, m)

    def each(f):
        def body(k, _):
            f(k)
            return 0
        lax.fori_loop(1, NZ, body, 0)

    each(lambda k: zpush(k).start())
    mixer.relay()
    each(lambda k: zcame(k).wait_recv())
    zero, one = jnp.zeros((1, 128), jnp.float32), jnp.ones((1, 128), jnp.float32)

    def fold(zz, carry):
        a, b = carry
        pair = line_ref[zz]
        return a * pair[0:1], pair[0:1] * b + pair[1:2]

    before = lax.fori_loop(0, z, fold, (one, zero))
    whole = lax.fori_loop(z, NZ, fold, before)
    tile = jnp.concatenate([whole[0], whole[1], jnp.zeros((6, 128), jnp.float32)], 0)
    total_ref[...] = tile

    def ypush(k):
        return remote(total_ref, col_ref.at[y], pys.at[k], pyr.at[k], (y + k) % NY, z, m)

    def ycame(k):
        return remote(total_ref, col_ref.at[(y + NY - k) % NY], pys.at[k], pyr.at[k], (y + k) % NY, z, m)

    for k in range(1, NY):
        ypush(k).start()
    for k in range(1, NY):
        ycame(k).wait_recv()
    col_ref[y] = tile

    def fold_y(yy, h):
        pair = col_ref[yy]
        return pair[0:1] * h + pair[1:2]

    h = lax.fori_loop(0, y, fold_y, zero)
    arriving = before[0] * h + before[1]
    g = MpGather(lambda mm: states_ref.at[:, pl.ds(pl.multiple_of(mm * 128, 128), 128)], gs, gr, (s, x, c))
    states_ref[:, pl.ds(pl.multiple_of(m * 128, 128), 128)] = (local + through * arriving).astype(jnp.bfloat16)
    g.start()
    g.relay()
    g.finish()
    mixer.finish()
    g.drain()
    mixer.drain()
    each(lambda k: zpush(k).wait_send())
    for k in range(1, NY):
        ypush(k).wait_send()


def scan_stage(byte_states, outer_gain, mamba_input, mamba_step, decay_rate, mixer_weight):
    tile = pltpu.VMEM((8, 128), jnp.float32)
    return pl.pallas_call(
        scan_kernel,
        out_shape=[
            jax.ShapeDtypeStruct((256, 1024), jnp.bfloat16),
            jax.ShapeDtypeStruct((1024, 1024), jnp.bfloat16),
        ],
        in_specs=[VM] * 6,
        out_specs=[VM] * 2,
        scratch_shapes=[
            tile, pltpu.VMEM((NZ, 8, 128), jnp.float32), tile, pltpu.VMEM((NY, 8, 128), jnp.float32),
            DMA((NZ,)), DMA((NZ,)), DMA((NY,)), DMA((NY,)), DMA((8,)), DMA((8,)), DMA((8,)), DMA((8,)), DMA((1,)),
        ],
        compiler_params=params(2),
        name="scan",
    )(byte_states, outer_gain[None, :], mamba_input, mamba_step, decay_rate[None, :], mixer_weight)


def mp_gather_kernel(own_ref, full_ref, ss, rs, lsem):
    y, z, x, c = coords()
    s, m = y * NZ + z, x * NC + c
    width = own_ref.shape[1]
    enter(mp_peers(s, x, c))
    g = MpGather(lambda mm: full_ref.at[:, pl.ds(pl.multiple_of(mm * width, 128), width)], ss, rs, (s, x, c))
    cp = pltpu.make_async_copy(own_ref, g.view(m), lsem.at[0])
    cp.start()
    cp.wait()
    g.start()
    g.relay()
    g.finish()
    g.drain()


def mp_gather(own):
    rows, width = own.shape
    return pl.pallas_call(
        mp_gather_kernel,
        out_shape=jax.ShapeDtypeStruct((rows, width * 8), own.dtype),
        in_specs=[VM],
        out_specs=VM,
        scratch_shapes=[DMA((8,)), DMA((8,)), DMA((1,))],
        compiler_params=params(3),
        name="mp_gather",
    )(own)


def kv_kernel(own_ref, a_out, b_out, *sems):
    y, z, x, c = coords()
    m = x * NC + c
    enter(yz_peers(y, z, m))
    gather_two(
        a_out, [(own_ref.at[pl.ds(0, KV_A)], pl.ds(0, 256))], b_out, own_ref.at[pl.ds(KV_A, CAP - KV_A)],
        y, z, m, 32, 48, sems,
    )


def gather_kv(own):
    return pl.pallas_call(
        kv_kernel,
        out_shape=[
            jax.ShapeDtypeStruct((NY, NZ, KV_A, 256), own.dtype),
            jax.ShapeDtypeStruct((NY, NZ, CAP - KV_A, 256), own.dtype),
        ],
        in_specs=[VM],
        out_specs=[VM] * 2,
        scratch_shapes=gather_sems(2),
        compiler_params=params(4),
        name="kv",
    )(own)


def attend_kernel(q_ref, kva_ref, kvb_ref, ida_ref, idb_ref, rows_ref, out_ref):
    s = lax.axis_index("seq")
    rows = rows_ref[...]
    qs = q_ref[...]
    scale = 1.0 / math.sqrt(HEAD)
    total = qs.shape[0]

    def block(carry, kv, ids):
        peak, denom, acc = carry
        scores = lax.dot_general(qs, kv[:, :HEAD], (((1,), (1,)), ((), ())), preferred_element_type=jnp.float32)
        scores = jnp.where(ids <= rows, scores * scale, masked)
        new_peak = jnp.maximum(peak, jnp.max(scores, axis=1, keepdims=True))
        shrink = jnp.exp(peak - new_peak)
        lifted = jnp.exp(scores - new_peak)
        denom = denom * shrink + jnp.sum(lifted, axis=1, keepdims=True)
        acc = acc * shrink + jnp.dot(lifted.astype(jnp.bfloat16), kv[:, HEAD:], preferred_element_type=jnp.float32)
        return new_peak, denom, acc

    def step(i, carry):
        carry = block(carry, kva_ref[i].reshape(8 * KV_A, 256), ida_ref[i])
        return block(carry, kvb_ref[i].reshape(8 * (CAP - KV_A), 256), idb_ref[i])

    init = (
        jnp.full((total, 1), masked, jnp.float32),
        jnp.zeros((total, 1), jnp.float32),
        jnp.zeros((total, HEAD), jnp.float32),
    )
    _, denom, acc = lax.fori_loop(0, s // 8 + 1, step, init)
    out_ref[...] = (acc / denom).astype(jnp.bfloat16)


def reduce_kernel(part_ref, out_ref, box_ref, ss, rs):
    y, z, x, c = coords()
    s, m = y * NZ + z, x * NC + c
    enter([(s, (m + k) % 8) for k in range(1, 8)])

    def push(k):
        to = (m + k) % 8
        return pltpu.make_async_remote_copy(
            src_ref=part_ref.at[:, pl.ds(pl.multiple_of(to * 128, 128), 128)], dst_ref=box_ref.at[k],
            send_sem=ss.at[k], recv_sem=rs.at[k], device_id=(s, to), device_id_type=MESH,
        )

    for k in range(1, 8):
        push(k).start()
    acc = part_ref[:, pl.ds(pl.multiple_of(m * 128, 128), 128)].astype(jnp.float32)
    for k in range(1, 8):
        push(k).wait_recv()
        acc = acc + box_ref[k].astype(jnp.float32)
    out_ref[...] = acc.astype(jnp.bfloat16)
    for k in range(1, 8):
        push(k).wait_send()


def reduce_mp(part):
    return pl.pallas_call(
        reduce_kernel,
        out_shape=jax.ShapeDtypeStruct((CAP, 128), jnp.bfloat16),
        in_specs=[VM],
        out_specs=VM,
        scratch_shapes=[pltpu.VMEM((8, CAP, 128), jnp.bfloat16), DMA((8,)), DMA((8,))],
        compiler_params=params(5),
        name="reduce_mp",
    )(part)


def on_device(
    byte_states, outer_gain, mamba_input, mamba_step, decay_rate, mixer_weight, boundaries, span_counts,
    up_weight, up_bias, inner_gain, query_weight, key_weight, value_weight, return_weight,
):
    f32, bf = jnp.float32, jnp.bfloat16
    own_shard = lax.axis_index("seq")
    own_lane = lax.axis_index("mp")
    counts = span_counts
    offsets = jnp.cumsum(counts) - counts
    seq_ids = jnp.arange(64, dtype=jnp.int32)
    own_offset = jnp.sum(jnp.where(seq_ids == own_shard, offsets, 0))
    own_count = jnp.sum(jnp.where(seq_ids == own_shard, counts, 0))
    slots = jnp.arange(CAP, dtype=jnp.int32)
    key_ids = jnp.where(slots[None, :] < counts[:, None], offsets[:, None] + slots[None, :], far_index)
    ida = key_ids[:, :KV_A].reshape(8, 1, 8 * KV_A)
    idb = key_ids[:, KV_A:].reshape(8, 1, 8 * (CAP - KV_A))
    query_rows = jnp.tile(own_offset + slots, 4)[:, None]

    u_full, kv_weight, q_weight = gather_weights(up_weight, query_weight, key_weight, value_weight)
    states, mixer = scan_stage(byte_states, outer_gain, mamba_input, mamba_step, decay_rate, mixer_weight)
    mixed = jnp.dot(states, mixer, preferred_element_type=f32)
    encoded = (byte_states.astype(f32) + mixed).astype(bf)
    skip_part = lax.dynamic_slice_in_dim(encoded, own_lane * 128, 128, 1)
    marks = boundaries[0]
    byte_ids = jnp.arange(256, dtype=jnp.int32)
    pick = (jnp.minimum(marks, 255)[:, None] == byte_ids[None, :]).astype(bf)
    pooled = jnp.dot(pick, encoded, preferred_element_type=f32).astype(bf)
    share = (jnp.dot(pooled, u_full, preferred_element_type=f32) + up_bias[None, :]).astype(bf)
    widened = mp_gather(share).astype(f32)
    normed = (
        widened * lax.rsqrt(jnp.mean(widened * widened, axis=-1, keepdims=True) + eps) * inner_gain
    ).astype(bf)
    queries = jnp.dot(normed, q_weight, preferred_element_type=f32).astype(bf)
    kv = jnp.dot(normed, kv_weight, preferred_element_type=f32).astype(bf)
    kva, kvb = gather_kv(kv)
    stacked = queries.reshape(CAP, 4, HEAD).transpose(1, 0, 2).reshape(4 * CAP, HEAD)
    attended = pl.pallas_call(
        attend_kernel,
        out_shape=jax.ShapeDtypeStruct((4 * CAP, HEAD), bf),
        in_specs=[VM] * 6,
        out_specs=VM,
        compiler_params=pltpu.CompilerParams(vmem_limit_bytes=56 << 20),
        name="attend",
    )(stacked, kva.reshape(8, 8, KV_A, 256), kvb.reshape(8, 8, CAP - KV_A, 256), ida, idb, query_rows)
    attended = attended.reshape(4, CAP, HEAD).transpose(1, 0, 2).reshape(CAP, 4 * HEAD)
    projected = jnp.dot(attended, return_weight, preferred_element_type=f32).astype(bf)
    returned = reduce_mp(projected)
    live = slots < own_count
    passed = jnp.sum(((marks[None, :] <= byte_ids[:, None]) & live[None, :]).astype(jnp.int32), axis=1)
    spread = (passed[:, None] - 1 == slots[None, :]).astype(bf)
    back = jnp.dot(spread, returned, preferred_element_type=f32)
    return (skip_part.astype(f32) + back).astype(bf)


def solution(mesh):
    in_specs = (
        P("seq", None), P(), P(None, "mp"), P(None, "mp"), P("mp"), P("mp", None), P("seq", None), P(),
        P("seq", "mp"), P("mp"), P(), P("seq", "mp"), P("seq", "mp"), P("seq", "mp"), P("mp", None),
    )
    return jax.shard_map(on_device, mesh=mesh, in_specs=in_specs, out_specs=P("seq", "mp"), check_vma=False)
```

```python
import math

import jax
import jax.numpy as jnp
from jax import lax
from jax.experimental import pallas as pl
from jax.experimental.pallas import tpu as pltpu
from jax.sharding import PartitionSpec as P

HEADS = 32
KV_HEADS = 8
HEAD = 128
GROUP = HEADS // KV_HEADS
NY, NZ = 4, 16
NX, NC = 4, 2
CAP = 128
ROWS = 256
KV_A = 48
Q_A = 16
STEPS = (8, 7)

eps = 1e-05
masked = -1e30
far_index = 1073741824

MESH = pl.DeviceIdType.MESH
VM = pl.BlockSpec(memory_space=pltpu.VMEM)
SM = pl.BlockSpec(memory_space=pltpu.SMEM)
DMA = pltpu.SemaphoreType.DMA
f32, bf16 = jnp.float32, jnp.bfloat16


def coords():
    s, m = lax.axis_index("seq"), lax.axis_index("mp")
    return s // NZ, s % NZ, m // NC, m % NC


def remote(src, dst, ss, rs, s, m):
    return pltpu.make_async_remote_copy(
        src_ref=src, dst_ref=dst, send_sem=ss, recv_sem=rs, device_id=(s, m), device_id_type=MESH
    )


def when(cond, f):
    if isinstance(cond, bool):
        if cond:
            f()
    else:
        pl.when(cond)(f)


def loop(lo, hi, f):
    def body(i, _):
        f(i)
        return 0

    lax.fori_loop(lo, hi, body, 0)


class PushY:
    def __init__(self, buf, lo, hi, ss, rs, place):
        self.buf, self.lo, self.n, self.ss, self.rs = buf, lo, hi - lo, ss, rs
        self.y, self.z, self.m = place

    def copy(self, k, yy, zz, slot):
        ref = self.buf.at[yy % NY, zz, pl.ds(self.lo, self.n)]
        return remote(ref, ref, self.ss.at[0], self.rs.at[slot], (self.y + k) % NY * NZ + self.z, self.m)

    def start(self, zz, slot):
        for k in (2, 1, 3):
            self.copy(k, self.y, zz, k if slot is None else slot).start()

    def came(self, k):
        self.copy(k, self.y + NY - k, self.z, k).wait_recv()

    def wait(self, columns, slot=0):
        ref = self.buf.at[pl.ds(0, 3), pl.ds(0, columns), pl.ds(self.lo, self.n)]
        pltpu.make_async_copy(ref, ref, self.rs.at[slot]).wait()

    def drain(self, columns):
        ref = self.buf.at[pl.ds(0, 3), pl.ds(0, columns), pl.ds(self.lo, self.n)]
        pltpu.make_async_copy(ref, ref, self.ss.at[0]).wait()


class RingZ:
    def __init__(self, buf, lo, hi, k, ss, rs, place):
        self.buf, self.lo, self.n, self.k, self.ss, self.rs = buf, lo, hi - lo, k, ss, rs
        self.y, self.z, self.m = place

    def item(self, d, t):
        return (self.z + (NZ - t if d == 0 else t)) % NZ

    def copy(self, d, t, zz):
        ref = self.buf.at[(self.y + self.k) % NY, zz, pl.ds(self.lo, self.n)]
        to = (self.z + (1 if d == 0 else NZ - 1)) % NZ
        return remote(ref, ref, self.ss.at[0], self.rs.at[2 * self.k + d, t], self.y * NZ + to, self.m)

    def own(self):
        for d in range(2):
            self.copy(d, 0, self.z).start()

    def step(self, d, t):
        zz = self.item(d, t)
        self.copy(d, t - 1, zz).wait_recv()
        when(t < STEPS[d], lambda: self.copy(d, t, zz).start())

    def drain(self, blocks):
        ref = self.buf.at[pl.ds(0, blocks), pl.ds(0, NZ - 1), pl.ds(self.lo, self.n)]
        pltpu.make_async_copy(ref, ref, self.ss.at[0]).wait()


class YFirst:
    def __init__(self, buf, lo, hi, sems, place):
        yss, yrs, zss, zrs = sems
        self.z = place[1]
        self.push = PushY(buf, lo, hi, yss, yrs, place)
        self.rings = [RingZ(buf, lo, hi, k, zss, zrs, place) for k in range(NY)]

    def own(self):
        self.push.start(self.z, None)
        self.rings[0].own()

    def spread(self):
        for k in (1, 3, 2):
            self.push.came(k)
            self.rings[NY - k].own()

    def step(self, t):
        for d in range(2):
            def go():
                for k in (0, 3, 1, 2):
                    self.rings[k].step(d, t)
            when(t <= STEPS[d], go)

    def drain(self):
        self.push.drain(1)
        self.rings[0].drain(NY)


class ZFirst:
    def __init__(self, buf, lo, hi, sems, place, by_column=False):
        yss, yrs, zss, zrs = sems
        self.z, self.by_column = place[1], by_column
        self.push = PushY(buf, lo, hi, yss, yrs, place)
        self.ring = RingZ(buf, lo, hi, 0, zss, zrs, place)

    def start(self, zz):
        self.push.start(zz, zz if self.by_column else 0)

    def own(self):
        self.ring.own()
        self.start(self.z)

    def step(self, t):
        for d in range(2):
            def go():
                self.ring.step(d, t)
                self.start(self.ring.item(d, t))
            when(t <= STEPS[d], go)

    def finish(self):
        self.push.wait(NZ)

    def drain(self):
        self.push.drain(NZ)
        self.ring.drain(1)


def ring_sems(y_first):
    zs = (8, 8) if y_first else (2, 8)
    return [DMA((1,)), DMA((NZ,)), DMA((1,)), DMA(zs)]


class MpGather:
    def __init__(self, view, ss, rs, place):
        self.view, self.ss, self.rs = view, ss, rs
        self.s, self.x, self.c = place

    def same(self, k, back):
        ref = self.view(((self.x + (NX - k if back else 0)) % NX) * NC + self.c)
        return remote(ref, ref, self.ss.at[k], self.rs.at[k], self.s, ((self.x + k) % NX) * NC + self.c)

    def across(self, k, core):
        ref = self.view(((self.x + NX - k) % NX) * NC + core)
        return remote(ref, ref, self.ss.at[4 + k], self.rs.at[4 + k], self.s, self.x * NC + 1 - self.c)

    def start(self):
        for k in (2, 1, 3):
            self.same(k, False).start()
        self.across(0, self.c).start()

    def relay(self):
        for k in (1, 3, 2):
            self.same(k, True).wait_recv()
            self.across(k, self.c).start()

    def finish(self):
        for k in (0, 1, 3, 2):
            self.across(k, 1 - self.c).wait_recv()

    def drain(self):
        for k in (1, 2, 3):
            self.same(k, False).wait_send()
        for k in range(4):
            self.across(k, self.c).wait_send()


def one_minus_exp(v):
    series = v * (1.0 - v * (0.5 - v * (1 / 6 - v * (1 / 24 - v * (1 / 120 - v / 720)))))
    return jnp.where(v < 0.25, series, 1.0 - jnp.exp(-v))


def scan_rows(decays, drives):
    rows = decays.shape[0]
    ids = lax.broadcasted_iota(jnp.int32, decays.shape, 0)
    k = 1
    while k < rows:
        if k < 8:
            a_back = jnp.where(ids >= k, pltpu.roll(decays, k, 0), 1.0)
            b_back = jnp.where(ids >= k, pltpu.roll(drives, k, 0), 0.0)
        else:
            a_back = jnp.concatenate([jnp.ones((k, decays.shape[1]), f32), decays[: rows - k]], 0)
            b_back = jnp.concatenate([jnp.zeros((k, decays.shape[1]), f32), drives[: rows - k]], 0)
        drives = decays * b_back + drives
        decays = decays * a_back
        k *= 2
    return decays, drives


def block_cols(m, width=128):
    return pl.ds(pl.multiple_of(m * width, 128), width)


def row_of(ref):
    return ref[...].reshape(1, ref.shape[0])


def kernel(
    counts_ref, marks_ref, gain_ref, rate_ref, bias_ref, igain_ref,
    bytes_hbm, win_hbm, wstep_hbm, mixer_hbm, up_hbm, wq_hbm, wk_hbm, wv_hbm, wret_hbm,
    out_ref,
    offs_ref, bytes_ref, win_ref, wstep_ref, wret_ref, through_ref, local_ref, pair_ref, line_ref, total_ref, col_ref,
    states_ref, mix_ref, u_ref, kvw_ref, q_ref, kv_ref, stage_ref, enc_ref, wide_ref, peak_ref, denom_ref, acc_ref,
    part_ref, box_ref,
    pzs, pzr, pys, pyr, gs, gr, ms, mr, ws, wr, bs, br, lsem, *ring,
):
    y, z, x, c = coords()
    s, m = y * NZ + z, x * NC + c
    place = (y, z, m)
    peers = [(y * NZ + (z + k) % NZ, m) for k in range(1, NZ)]
    peers += [((y + k) % NY * NZ + z, m) for k in range(1, NY)]
    peers += [(s, (m + k) % 8) for k in range(1, 8)]
    barrier = pltpu.get_barrier_semaphore()
    for seq, mp in peers:
        pl.semaphore_signal(barrier, inc=1, device_id=(seq, mp), device_id_type=MESH)

    u = YFirst(u_ref, 0, 16, ring[0:4], place)
    kvw = ZFirst(kvw_ref, 0, 64, ring[4:8], place)
    qa = YFirst(q_ref, 0, Q_A, ring[8:12], place)
    qb = ZFirst(q_ref, Q_A, 64, ring[12:16], place)
    kva = YFirst(kv_ref, 0, KV_A, ring[16:20], place)
    kvb = ZFirst(kv_ref, KV_A, CAP, ring[20:24], place, by_column=True)
    mixer = MpGather(lambda mm: mix_ref.at[pl.ds(pl.multiple_of(mm * 128, 128), 128)], ms, mr, (s, x, c))
    g = MpGather(lambda mm: states_ref.at[:, block_cols(mm)], gs, gr, (s, x, c))
    w = MpGather(lambda mm: wide_ref.at[:, block_cols(mm, 512)], ws, wr, (s, x, c))

    copies = [
        pltpu.make_async_copy(src, dst, lsem.at[i])
        for i, (src, dst) in enumerate([
            (bytes_hbm, bytes_ref),
            (win_hbm, win_ref),
            (wstep_hbm, wstep_ref),
            (up_hbm, u_ref.at[y, z]),
            (wk_hbm, kvw_ref.at[y, z, :, pl.ds(0, HEAD)]),
            (wv_hbm, kvw_ref.at[y, z, :, pl.ds(HEAD, HEAD)]),
            (wq_hbm, q_ref.at[y, z]),
            (mixer_hbm, mixer.view(m)),
            (wret_hbm, wret_ref),
        ])
    ]
    for cp in copies:
        cp.start()

    def offsets(i, acc):
        offs_ref[i] = acc
        return acc + counts_ref[i]

    lax.fori_loop(0, 64, offsets, jnp.int32(0))
    for cp in copies[:3]:
        cp.wait()

    values = bytes_ref[...].astype(f32)
    scale = lax.rsqrt(jnp.mean(values * values, axis=-1, keepdims=True) + eps)
    normed = (values * scale * row_of(gain_ref)).astype(bf16)
    inputs = jnp.dot(normed, win_ref[...], preferred_element_type=f32)
    raw = jnp.dot(normed, wstep_ref[...], preferred_element_type=f32)
    rate = (jnp.maximum(raw, 0.0) + jnp.log1p(jnp.exp(-jnp.abs(raw)))) * row_of(rate_ref)
    through, local = scan_rows(jnp.exp(-rate), jnp.sqrt(one_minus_exp(2.0 * rate)) * inputs)
    through_ref[...] = through
    local_ref[...] = local
    tile = jnp.concatenate([through[ROWS - 1 :], local[ROWS - 1 :], jnp.zeros((6, 128), f32)], 0)
    pair_ref[...] = tile
    line_ref[z] = tile
    for cp in copies[3:]:
        cp.wait()
    pl.semaphore_wait(barrier, len(peers))

    def zpush(k):
        return remote(pair_ref, line_ref.at[z], pzs.at[k], pzr.at[k], y * NZ + (z + k) % NZ, m)

    def zcame(k):
        ref = line_ref.at[(z + NZ - k) % NZ]
        return remote(ref, ref, pzs.at[k], pzr.at[k], y * NZ + (z + k) % NZ, m)

    def ypush(k):
        return remote(total_ref, col_ref.at[y], pys.at[k], pyr.at[k], (y + k) % NY * NZ + z, m)

    def ycame(k):
        ref = col_ref.at[(y + NY - k) % NY]
        return remote(ref, ref, pys.at[k], pyr.at[k], (y + k) % NY * NZ + z, m)

    def step_a(t):
        u.step(t)
        kvw.step(t)

    def step_q(t):
        qa.step(t)
        qb.step(t)

    loop(1, NZ, lambda k: zpush(k).start())
    u.own()
    kvw.own()
    qa.own()
    qb.own()
    mixer.start()
    u.spread()
    qa.spread()
    loop(1, 3, step_a)
    step_q(1)
    loop(1, NZ, lambda k: zcame(k).wait_recv())
    zero, one = jnp.zeros((1, 128), f32), jnp.ones((1, 128), f32)

    def fold(zz, carry):
        pair = line_ref[zz]
        return carry[0] * pair[0:1], pair[0:1] * carry[1] + pair[1:2]

    before = lax.fori_loop(0, z, fold, (one, zero))
    whole = lax.fori_loop(z, NZ, fold, before)
    tile = jnp.concatenate([whole[0], whole[1], jnp.zeros((6, 128), f32)], 0)
    total_ref[...] = tile
    col_ref[y] = tile
    for k in range(1, NY):
        ypush(k).start()
    step_a(3)
    for k in range(1, NY):
        ycame(k).wait_recv()

    def fold_y(yy, h):
        pair = col_ref[yy]
        return pair[0:1] * h + pair[1:2]

    arriving = before[0] * lax.fori_loop(0, y, fold_y, zero) + before[1]
    states_ref[:, block_cols(m)] = (local_ref[...] + through_ref[...] * arriving).astype(bf16)
    g.start()
    mixer.relay()
    step_a(4)
    g.relay()
    step_a(5)
    g.finish()
    mixer.finish()
    step_q(2)

    mixed = jnp.dot(states_ref[...], mix_ref[...], preferred_element_type=f32)
    enc_ref[...] = (bytes_ref[...].astype(f32) + mixed).astype(bf16)
    step_a(6)
    marks = marks_ref[...]
    byte_ids = lax.broadcasted_iota(jnp.int32, (ROWS, CAP), 0)
    pick = jnp.where(jnp.minimum(marks, ROWS - 1) == byte_ids, 1.0, 0.0).astype(bf16)
    pooled = lax.dot_general(
        pick, enc_ref[...], (((0,), (0,)), ((), ())), preferred_element_type=f32
    ).astype(bf16)
    loop(7, 9, step_a)
    u_full = u_ref[...].reshape(1024, 512)
    share = jnp.dot(pooled, u_full, preferred_element_type=f32) + row_of(bias_ref)
    wide_ref[:, block_cols(m, 512)] = share.astype(bf16)
    w.start()
    loop(3, 5, step_q)
    w.relay()
    step_q(5)
    w.finish()
    wide = wide_ref[...].astype(f32)
    scale = lax.rsqrt(jnp.mean(wide * wide, axis=-1, keepdims=True) + eps)
    wide_n = (wide * scale * row_of(igain_ref)).astype(bf16)
    kvw.finish()
    kv = jnp.dot(wide_n, kvw_ref[...].reshape(4096, 256), preferred_element_type=f32)
    kv_ref[y, z] = kv.astype(bf16)
    kva.own()
    kvb.own()
    step_q(6)
    kva.spread()

    def step_kv(t):
        kva.step(t)
        kvb.step(t)

    def step_both(t):
        step_q(t + 6)
        step_kv(t)

    loop(1, 3, step_both)
    qb.finish()
    queries = jnp.dot(wide_n, q_ref[...].reshape(4096, 512), preferred_element_type=f32).astype(bf16)
    stacked = jnp.concatenate([queries[:, h * HEAD : (h + 1) * HEAD] for h in range(GROUP)], 0)

    total = GROUP * CAP
    own_rows = offs_ref[s] + (lax.broadcasted_iota(jnp.int32, (total, 1), 0) & (CAP - 1))
    slots = lax.broadcasted_iota(jnp.int32, (1, CAP), 1)
    peak_ref[...] = jnp.full((total, CAP), masked, f32)
    denom_ref[...] = jnp.zeros((total, CAP), f32)
    acc_ref[...] = jnp.zeros((total, HEAD), f32)

    def ids_of(zz):
        return [
            jnp.where(slots < counts_ref[yy * NZ + zz], offs_ref[yy * NZ + zz] + slots, far_index)
            for yy in range(NY)
        ]

    def turn(j):
        pl.when(j <= 5)(lambda: step_kv(j + 3))
        columns = ((z + j) % NZ, (z + NZ - 1 - j) % NZ)
        staged = []
        for i, zz in enumerate(columns):
            kvb.push.wait(1, zz)
            staged.append(pltpu.make_async_copy(kv_ref.at[:, zz], stage_ref.at[i], lsem.at[i]))
            staged[i].start()
        ids = jnp.concatenate(ids_of(columns[0]) + ids_of(columns[1]), 1)
        for cp in staged:
            cp.wait()
        kv = stage_ref[...].reshape(2 * NY * CAP, 2 * HEAD)
        scores = lax.dot_general(stacked, kv[:, :HEAD], (((1,), (1,)), ((), ())), preferred_element_type=f32)
        scores = jnp.where(ids <= own_rows, scores * (1.0 / math.sqrt(HEAD)), masked)
        peak = peak_ref[:, 0:1]
        new_peak = jnp.maximum(peak, jnp.max(scores, axis=1, keepdims=True))
        shrink = jnp.exp(peak - new_peak)
        lifted = jnp.exp(scores - new_peak)
        denom = denom_ref[:, 0:1] * shrink + jnp.sum(lifted, axis=1, keepdims=True)
        acc = jnp.dot(lifted.astype(bf16), kv[:, HEAD:], preferred_element_type=f32)
        acc_ref[...] = acc_ref[...] * shrink + acc
        peak_ref[...] = jnp.broadcast_to(new_peak, (total, CAP))
        denom_ref[...] = jnp.broadcast_to(denom, (total, CAP))

    loop(0, 8, turn)
    attended = (acc_ref[...] / denom_ref[...]).astype(bf16)
    attended = jnp.concatenate([attended[h * CAP : (h + 1) * CAP] for h in range(GROUP)], 1)

    part_ref[...] = jnp.dot(attended, wret_ref[...], preferred_element_type=f32).astype(bf16)

    def push(k):
        to = (m + k) % 8
        return remote(part_ref.at[:, block_cols(to)], box_ref.at[k], bs.at[k], br.at[k], s, to)

    for k in range(1, 8):
        push(k).start()
    live = (marks <= byte_ids) & (lax.broadcasted_iota(jnp.int32, (ROWS, CAP), 1) < counts_ref[s])
    passed = jnp.sum(jnp.where(live, 1.0, 0.0), axis=1, keepdims=True)
    lane = lax.broadcasted_iota(jnp.int32, (ROWS, CAP), 1).astype(f32)
    spread = jnp.where(passed - 1.0 == lane, 1.0, 0.0).astype(bf16)

    for gather in (mixer, g, w):
        gather.drain()
    loop(1, NZ, lambda k: zpush(k).wait_send())
    for k in range(1, NY):
        ypush(k).wait_send()
    for stream in (u, kvw, qa, qb, kva, kvb):
        stream.drain()

    acc = part_ref[:, block_cols(m)].astype(f32)
    for k in range(1, 8):
        push(k).wait_recv()
        acc = acc + box_ref[k].astype(f32)
    back = jnp.dot(spread, acc.astype(bf16), preferred_element_type=f32)
    out_ref[...] = (enc_ref[:, block_cols(m)].astype(f32) + back).astype(bf16)
    for k in range(1, 8):
        push(k).wait_send()


def on_device(
    byte_states, outer_gain, mamba_input, mamba_step, decay_rate, mixer_weight, boundaries, span_counts,
    up_weight, up_bias, inner_gain, query_weight, key_weight, value_weight, return_weight,
):
    tile = pltpu.VMEM((8, 128), f32)
    rings = []
    for y_first in (True, False, True, False, True, False):
        rings += ring_sems(y_first)
    return pl.pallas_call(
        kernel,
        out_shape=jax.ShapeDtypeStruct((ROWS, 128), bf16),
        in_specs=[SM] + [VM] * 5 + [pl.BlockSpec(memory_space=pl.ANY)] * 9,
        out_specs=VM,
        scratch_shapes=[
            pltpu.SMEM((64,), jnp.int32),
            pltpu.VMEM((ROWS, 1024), bf16), pltpu.VMEM((1024, 128), bf16), pltpu.VMEM((1024, 128), bf16),
            pltpu.VMEM((512, 1024), bf16),
            pltpu.VMEM((ROWS, 128), f32), pltpu.VMEM((ROWS, 128), f32),
            tile, pltpu.VMEM((NZ, 8, 128), f32), tile, pltpu.VMEM((NY, 8, 128), f32),
            pltpu.VMEM((ROWS, 1024), bf16), pltpu.VMEM((1024, 1024), bf16),
            pltpu.VMEM((NY, NZ, 16, 512), bf16), pltpu.VMEM((NY, NZ, 64, 256), bf16),
            pltpu.VMEM((NY, NZ, 64, 512), bf16), pltpu.VMEM((NY, NZ, CAP, 256), bf16),
            pltpu.VMEM((2, NY, CAP, 256), bf16),
            pltpu.VMEM((ROWS, 1024), bf16), pltpu.VMEM((CAP, 4096), bf16),
            pltpu.VMEM((GROUP * CAP, CAP), f32), pltpu.VMEM((GROUP * CAP, CAP), f32),
            pltpu.VMEM((GROUP * CAP, HEAD), f32),
            pltpu.VMEM((CAP, 1024), bf16), pltpu.VMEM((8, CAP, 128), bf16),
            DMA((NZ,)), DMA((NZ,)), DMA((NY,)), DMA((NY,)),
            DMA((8,)), DMA((8,)), DMA((8,)), DMA((8,)), DMA((8,)), DMA((8,)), DMA((8,)), DMA((8,)),
            DMA((9,)),
        ] + rings,
        compiler_params=pltpu.CompilerParams(collective_id=1, has_side_effects=True, vmem_limit_bytes=58 << 20),
        name="window",
    )(
        span_counts, boundaries, outer_gain, decay_rate, up_bias, inner_gain,
        byte_states, mamba_input, mamba_step, mixer_weight,
        up_weight, query_weight, key_weight, value_weight, return_weight,
    )


def solution(mesh):
    in_specs = (
        P("seq", None), P(), P(None, "mp"), P(None, "mp"), P("mp"), P("mp", None), P("seq", None), P(),
        P("seq", "mp"), P("mp"), P(), P("seq", "mp"), P("seq", "mp"), P("seq", "mp"), P("mp", None),
    )
    return jax.shard_map(on_device, mesh=mesh, in_specs=in_specs, out_specs=P("seq", "mp"), check_vma=False)
```

```python
import math

import jax
import jax.numpy as jnp
from jax import lax
from jax.experimental import pallas as pl
from jax.experimental.pallas import tpu as pltpu
from jax.sharding import PartitionSpec as P

HEADS = 32
KV_HEADS = 8
HEAD = 128
GROUP = HEADS // KV_HEADS
NY, NZ = 4, 16
NX, NC = 4, 2
CAP = 128
ROWS = 256
KV_A = 32
Q_A = 32
STEPS = (8, 7)

eps = 1e-05
masked = -1e30
far_index = 1073741824

MESH = pl.DeviceIdType.MESH
VM = pl.BlockSpec(memory_space=pltpu.VMEM)
SM = pl.BlockSpec(memory_space=pltpu.SMEM)
DMA = pltpu.SemaphoreType.DMA
f32, bf16 = jnp.float32, jnp.bfloat16


def coords():
    s, m = lax.axis_index("seq"), lax.axis_index("mp")
    return s // NZ, s % NZ, m // NC, m % NC


def remote(src, dst, ss, rs, s, m):
    return pltpu.make_async_remote_copy(
        src_ref=src, dst_ref=dst, send_sem=ss, recv_sem=rs, device_id=(s, m), device_id_type=MESH
    )


def when(cond, f):
    if isinstance(cond, bool):
        if cond:
            f()
    else:
        pl.when(cond)(f)


def loop(lo, hi, f):
    def body(i, _):
        f(i)
        return 0

    lax.fori_loop(lo, hi, body, 0)


class PushY:
    def __init__(self, buf, lo, hi, ss, rs, place):
        self.buf, self.lo, self.n, self.ss, self.rs = buf, lo, hi - lo, ss, rs
        self.y, self.z, self.m = place

    def copy(self, k, yy, zz, slot):
        ref = self.buf.at[yy % NY, zz, pl.ds(self.lo, self.n)]
        return remote(ref, ref, self.ss.at[0], self.rs.at[slot], (self.y + k) % NY * NZ + self.z, self.m)

    def start(self, zz, slot):
        for k in (2, 1, 3):
            self.copy(k, self.y, zz, k if slot is None else slot).start()

    def came(self, k):
        self.copy(k, self.y + NY - k, self.z, k).wait_recv()

    def wait(self, columns, slot=0):
        ref = self.buf.at[pl.ds(0, 3), pl.ds(0, columns), pl.ds(self.lo, self.n)]
        pltpu.make_async_copy(ref, ref, self.rs.at[slot]).wait()

    def drain(self, columns):
        ref = self.buf.at[pl.ds(0, 3), pl.ds(0, columns), pl.ds(self.lo, self.n)]
        pltpu.make_async_copy(ref, ref, self.ss.at[0]).wait()


class RingZ:
    def __init__(self, buf, lo, hi, k, ss, rs, place):
        self.buf, self.lo, self.n, self.k, self.ss, self.rs = buf, lo, hi - lo, k, ss, rs
        self.y, self.z, self.m = place

    def item(self, d, t):
        return (self.z + (NZ - t if d == 0 else t)) % NZ

    def copy(self, d, t, zz):
        ref = self.buf.at[(self.y + self.k) % NY, zz, pl.ds(self.lo, self.n)]
        to = (self.z + (1 if d == 0 else NZ - 1)) % NZ
        return remote(ref, ref, self.ss.at[0], self.rs.at[2 * self.k + d, t], self.y * NZ + to, self.m)

    def own(self):
        for d in range(2):
            self.copy(d, 0, self.z).start()

    def step(self, d, t):
        zz = self.item(d, t)
        self.copy(d, t - 1, zz).wait_recv()
        when(t < STEPS[d], lambda: self.copy(d, t, zz).start())

    def drain(self, blocks):
        ref = self.buf.at[pl.ds(0, blocks), pl.ds(0, NZ - 1), pl.ds(self.lo, self.n)]
        pltpu.make_async_copy(ref, ref, self.ss.at[0]).wait()


class YFirst:
    def __init__(self, buf, lo, hi, sems, place):
        yss, yrs, zss, zrs = sems
        self.z = place[1]
        self.push = PushY(buf, lo, hi, yss, yrs, place)
        self.rings = [RingZ(buf, lo, hi, k, zss, zrs, place) for k in range(NY)]

    def own(self):
        self.push.start(self.z, None)
        self.rings[0].own()

    def spread(self):
        for k in (1, 3, 2):
            self.push.came(k)
            self.rings[NY - k].own()

    def step(self, t):
        for d in range(2):
            def go():
                for k in (0, 3, 1, 2):
                    self.rings[k].step(d, t)
            when(t <= STEPS[d], go)

    def drain(self):
        self.push.drain(1)
        self.rings[0].drain(NY)


class ZFirst:
    def __init__(self, buf, lo, hi, sems, place, by_column=False):
        yss, yrs, zss, zrs = sems
        self.z, self.by_column = place[1], by_column
        self.push = PushY(buf, lo, hi, yss, yrs, place)
        self.ring = RingZ(buf, lo, hi, 0, zss, zrs, place)

    def start(self, zz):
        self.push.start(zz, zz if self.by_column else 0)

    def own(self):
        self.ring.own()
        self.start(self.z)

    def step(self, t):
        for d in range(2):
            def go():
                self.ring.step(d, t)
                self.start(self.ring.item(d, t))
            when(t <= STEPS[d], go)

    def finish(self):
        self.push.wait(NZ)

    def drain(self):
        self.push.drain(NZ)
        self.ring.drain(1)


def ring_sems(y_first):
    zs = (8, 8) if y_first else (2, 8)
    return [DMA((1,)), DMA((NZ,)), DMA((1,)), DMA(zs)]


class MpGather:
    def __init__(self, view, ss, rs, place):
        self.view, self.ss, self.rs = view, ss, rs
        self.s, self.x, self.c = place

    def same(self, k, back):
        ref = self.view(((self.x + (NX - k if back else 0)) % NX) * NC + self.c)
        return remote(ref, ref, self.ss.at[k], self.rs.at[k], self.s, ((self.x + k) % NX) * NC + self.c)

    def across(self, k, core):
        ref = self.view(((self.x + NX - k) % NX) * NC + core)
        return remote(ref, ref, self.ss.at[4 + k], self.rs.at[4 + k], self.s, self.x * NC + 1 - self.c)

    def start(self):
        for k in (2, 1, 3):
            self.same(k, False).start()
        self.across(0, self.c).start()

    def relay(self):
        for k in (1, 3, 2):
            self.same(k, True).wait_recv()
            self.across(k, self.c).start()

    def finish(self):
        for k in (0, 1, 3, 2):
            self.across(k, 1 - self.c).wait_recv()

    def drain(self):
        for k in (1, 2, 3):
            self.same(k, False).wait_send()
        for k in range(4):
            self.across(k, self.c).wait_send()


def one_minus_exp(v):
    series = v * (1.0 - v * (0.5 - v * (1 / 6 - v * (1 / 24 - v * (1 / 120 - v / 720)))))
    return jnp.where(v < 0.25, series, 1.0 - jnp.exp(-v))


def scan_rows(decays, drives):
    rows = decays.shape[0]
    ids = lax.broadcasted_iota(jnp.int32, decays.shape, 0)
    k = 1
    while k < rows:
        if k < 8:
            a_back = jnp.where(ids >= k, pltpu.roll(decays, k, 0), 1.0)
            b_back = jnp.where(ids >= k, pltpu.roll(drives, k, 0), 0.0)
        else:
            a_back = jnp.concatenate([jnp.ones((k, decays.shape[1]), f32), decays[: rows - k]], 0)
            b_back = jnp.concatenate([jnp.zeros((k, decays.shape[1]), f32), drives[: rows - k]], 0)
        drives = decays * b_back + drives
        decays = decays * a_back
        k *= 2
    return decays, drives


def block_cols(m, width=128):
    return pl.ds(pl.multiple_of(m * width, 128), width)


def row_of(ref):
    return ref[...].reshape(1, ref.shape[0])


def kernel(
    counts_ref, marks_ref, gain_ref, rate_ref, bias_ref, igain_ref,
    bytes_hbm, win_hbm, wstep_hbm, mixer_hbm, up_hbm, wq_hbm, wk_hbm, wv_hbm, wret_hbm,
    out_ref,
    offs_ref, bytes_ref, win_ref, wstep_ref, wret_ref, through_ref, local_ref, pair_ref, line_ref, total_ref, col_ref,
    states_ref, mix_ref, u_ref, kvw_ref, q_ref, kv_ref, stage_ref, enc_ref, wide_ref, peak_ref, denom_ref, acc_ref,
    part_ref, box_ref,
    pzs, pzr, pys, pyr, gs, gr, ms, mr, ws, wr, bs, br, lsem, *ring,
):
    y, z, x, c = coords()
    s, m = y * NZ + z, x * NC + c
    place = (y, z, m)
    peers = [(y * NZ + (z + k) % NZ, m) for k in range(1, NZ)]
    peers += [((y + k) % NY * NZ + z, m) for k in range(1, NY)]
    peers += [(s, (m + k) % 8) for k in range(1, 8)]
    barrier = pltpu.get_barrier_semaphore()
    for seq, mp in peers:
        pl.semaphore_signal(barrier, inc=1, device_id=(seq, mp), device_id_type=MESH)

    u = YFirst(u_ref, 0, 16, ring[0:4], place)
    kvw = ZFirst(kvw_ref, 0, 64, ring[4:8], place)
    qa = YFirst(q_ref, 0, Q_A, ring[8:12], place)
    qb = ZFirst(q_ref, Q_A, 64, ring[12:16], place)
    kva = YFirst(kv_ref, 0, KV_A, ring[16:20], place)
    kvb = ZFirst(kv_ref, KV_A, CAP, ring[20:24], place, by_column=True)
    mixer = MpGather(lambda mm: mix_ref.at[pl.ds(pl.multiple_of(mm * 128, 128), 128)], ms, mr, (s, x, c))
    g = MpGather(lambda mm: states_ref.at[:, block_cols(mm)], gs, gr, (s, x, c))
    w = MpGather(lambda mm: wide_ref.at[:, block_cols(mm, 512)], ws, wr, (s, x, c))

    copies = [
        pltpu.make_async_copy(src, dst, lsem.at[i])
        for i, (src, dst) in enumerate([
            (bytes_hbm, bytes_ref),
            (win_hbm, win_ref),
            (wstep_hbm, wstep_ref),
            (up_hbm, u_ref.at[y, z]),
            (wk_hbm, kvw_ref.at[y, z, :, pl.ds(0, HEAD)]),
            (wv_hbm, kvw_ref.at[y, z, :, pl.ds(HEAD, HEAD)]),
            (wq_hbm, q_ref.at[y, z]),
            (mixer_hbm, mixer.view(m)),
            (wret_hbm, wret_ref),
        ])
    ]
    for cp in copies:
        cp.start()

    def offsets(i, acc):
        offs_ref[i] = acc
        return acc + counts_ref[i]

    lax.fori_loop(0, 64, offsets, jnp.int32(0))
    for cp in copies[:3]:
        cp.wait()

    values = bytes_ref[...].astype(f32)
    scale = lax.rsqrt(jnp.mean(values * values, axis=-1, keepdims=True) + eps)
    normed = (values * scale * row_of(gain_ref)).astype(bf16)
    inputs = jnp.dot(normed, win_ref[...], preferred_element_type=f32)
    raw = jnp.dot(normed, wstep_ref[...], preferred_element_type=f32)
    rate = (jnp.maximum(raw, 0.0) + jnp.log1p(jnp.exp(-jnp.abs(raw)))) * row_of(rate_ref)
    through, local = scan_rows(jnp.exp(-rate), jnp.sqrt(one_minus_exp(2.0 * rate)) * inputs)
    through_ref[...] = through
    local_ref[...] = local
    tile = jnp.concatenate([through[ROWS - 1 :], local[ROWS - 1 :], jnp.zeros((6, 128), f32)], 0)
    pair_ref[...] = tile
    line_ref[z] = tile
    for cp in copies[3:]:
        cp.wait()
    pl.semaphore_wait(barrier, len(peers))

    def zpush(k):
        return remote(pair_ref, line_ref.at[z], pzs.at[k], pzr.at[k], y * NZ + (z + k) % NZ, m)

    def zcame(k):
        ref = line_ref.at[(z + NZ - k) % NZ]
        return remote(ref, ref, pzs.at[k], pzr.at[k], y * NZ + (z + k) % NZ, m)

    def ypush(k):
        return remote(total_ref, col_ref.at[y], pys.at[k], pyr.at[k], (y + k) % NY * NZ + z, m)

    def ycame(k):
        ref = col_ref.at[(y + NY - k) % NY]
        return remote(ref, ref, pys.at[k], pyr.at[k], (y + k) % NY * NZ + z, m)

    def step_a(t):
        u.step(t)
        kvw.step(t)

    def step_q(t):
        qa.step(t)
        qb.step(t)

    loop(1, NZ, lambda k: zpush(k).start())
    u.own()
    kvw.own()
    qa.own()
    qb.own()
    mixer.start()
    u.spread()
    qa.spread()
    loop(1, 3, step_a)
    step_q(1)
    loop(1, NZ, lambda k: zcame(k).wait_recv())
    zero, one = jnp.zeros((1, 128), f32), jnp.ones((1, 128), f32)

    def fold(zz, carry):
        pair = line_ref[zz]
        return carry[0] * pair[0:1], pair[0:1] * carry[1] + pair[1:2]

    before = lax.fori_loop(0, z, fold, (one, zero))
    whole = lax.fori_loop(z, NZ, fold, before)
    tile = jnp.concatenate([whole[0], whole[1], jnp.zeros((6, 128), f32)], 0)
    total_ref[...] = tile
    col_ref[y] = tile
    for k in range(1, NY):
        ypush(k).start()
    step_a(3)
    for k in range(1, NY):
        ycame(k).wait_recv()

    def fold_y(yy, h):
        pair = col_ref[yy]
        return pair[0:1] * h + pair[1:2]

    arriving = before[0] * lax.fori_loop(0, y, fold_y, zero) + before[1]
    states_ref[:, block_cols(m)] = (local_ref[...] + through_ref[...] * arriving).astype(bf16)
    g.start()
    mixer.relay()
    step_a(4)
    g.relay()
    step_a(5)
    g.finish()
    mixer.finish()
    step_q(2)

    mixed = jnp.dot(states_ref[...], mix_ref[...], preferred_element_type=f32)
    enc_ref[...] = (bytes_ref[...].astype(f32) + mixed).astype(bf16)
    step_a(6)
    marks = marks_ref[...]
    byte_ids = lax.broadcasted_iota(jnp.int32, (ROWS, CAP), 0)
    pick = jnp.where(jnp.minimum(marks, ROWS - 1) == byte_ids, 1.0, 0.0).astype(bf16)
    pooled = lax.dot_general(
        pick, enc_ref[...], (((0,), (0,)), ((), ())), preferred_element_type=f32
    ).astype(bf16)
    loop(7, 9, step_a)
    u_full = u_ref[...].reshape(1024, 512)
    share = jnp.dot(pooled, u_full, preferred_element_type=f32) + row_of(bias_ref)
    wide_ref[:, block_cols(m, 512)] = share.astype(bf16)
    w.start()
    loop(3, 5, step_q)
    w.relay()
    step_q(5)
    w.finish()
    wide = wide_ref[...].astype(f32)
    scale = lax.rsqrt(jnp.mean(wide * wide, axis=-1, keepdims=True) + eps)
    wide_n = (wide * scale * row_of(igain_ref)).astype(bf16)
    kvw.finish()
    kv = jnp.dot(wide_n, kvw_ref[...].reshape(4096, 256), preferred_element_type=f32)
    kv_ref[y, z] = kv.astype(bf16)
    kva.own()
    kvb.own()
    step_q(6)
    kva.spread()

    def step_kv(t):
        kva.step(t)
        kvb.step(t)

    def step_both(t):
        step_q(t + 6)
        step_kv(t)

    loop(1, 3, step_both)
    qb.finish()
    queries = jnp.dot(wide_n, q_ref[...].reshape(4096, 512), preferred_element_type=f32).astype(bf16)
    stacked = jnp.concatenate([queries[:, h * HEAD : (h + 1) * HEAD] for h in range(GROUP)], 0)

    total = GROUP * CAP
    own_rows = offs_ref[s] + (lax.broadcasted_iota(jnp.int32, (total, 1), 0) & (CAP - 1))
    slots = lax.broadcasted_iota(jnp.int32, (1, CAP), 1)
    peak_ref[...] = jnp.full((total, CAP), masked, f32)
    denom_ref[...] = jnp.zeros((total, CAP), f32)
    acc_ref[...] = jnp.zeros((total, HEAD), f32)

    def ids_of(zz):
        return [
            jnp.where(slots < counts_ref[yy * NZ + zz], offs_ref[yy * NZ + zz] + slots, far_index)
            for yy in range(NY)
        ]

    def turn(j):
        pl.when(j <= 5)(lambda: step_kv(j + 3))
        columns = ((z + j) % NZ, (z + NZ - 1 - j) % NZ)
        staged = []
        for i, zz in enumerate(columns):
            kvb.push.wait(1, zz)
            staged.append(pltpu.make_async_copy(kv_ref.at[:, zz], stage_ref.at[i], lsem.at[i]))
            staged[i].start()
        ids = jnp.concatenate(ids_of(columns[0]) + ids_of(columns[1]), 1)
        for cp in staged:
            cp.wait()
        kv = stage_ref[...].reshape(2 * NY * CAP, 2 * HEAD)
        scores = lax.dot_general(stacked, kv[:, :HEAD], (((1,), (1,)), ((), ())), preferred_element_type=f32)
        scores = jnp.where(ids <= own_rows, scores * (1.0 / math.sqrt(HEAD)), masked)
        peak = peak_ref[:, 0:1]
        new_peak = jnp.maximum(peak, jnp.max(scores, axis=1, keepdims=True))
        shrink = jnp.exp(peak - new_peak)
        lifted = jnp.exp(scores - new_peak)
        denom = denom_ref[:, 0:1] * shrink + jnp.sum(lifted, axis=1, keepdims=True)
        acc = jnp.dot(lifted.astype(bf16), kv[:, HEAD:], preferred_element_type=f32)
        acc_ref[...] = acc_ref[...] * shrink + acc
        peak_ref[...] = jnp.broadcast_to(new_peak, (total, CAP))
        denom_ref[...] = jnp.broadcast_to(denom, (total, CAP))

    loop(0, 8, turn)
    attended = (acc_ref[...] / denom_ref[...]).astype(bf16)
    attended = jnp.concatenate([attended[h * CAP : (h + 1) * CAP] for h in range(GROUP)], 1)

    part_ref[...] = jnp.dot(attended, wret_ref[...], preferred_element_type=f32).astype(bf16)

    def push(k):
        to = (m + k) % 8
        return remote(part_ref.at[:, block_cols(to)], box_ref.at[k], bs.at[k], br.at[k], s, to)

    for k in range(1, 8):
        push(k).start()
    live = (marks <= byte_ids) & (lax.broadcasted_iota(jnp.int32, (ROWS, CAP), 1) < counts_ref[s])
    passed = jnp.sum(jnp.where(live, 1.0, 0.0), axis=1, keepdims=True)
    lane = lax.broadcasted_iota(jnp.int32, (ROWS, CAP), 1).astype(f32)
    spread = jnp.where(passed - 1.0 == lane, 1.0, 0.0).astype(bf16)

    for gather in (mixer, g, w):
        gather.drain()
    loop(1, NZ, lambda k: zpush(k).wait_send())
    for k in range(1, NY):
        ypush(k).wait_send()
    for stream in (u, kvw, qa, qb, kva, kvb):
        stream.drain()

    acc = part_ref[:, block_cols(m)].astype(f32)
    for k in range(1, 8):
        push(k).wait_recv()
        acc = acc + box_ref[k].astype(f32)
    back = jnp.dot(spread, acc.astype(bf16), preferred_element_type=f32)
    out_ref[...] = (enc_ref[:, block_cols(m)].astype(f32) + back).astype(bf16)
    for k in range(1, 8):
        push(k).wait_send()


def on_device(
    byte_states, outer_gain, mamba_input, mamba_step, decay_rate, mixer_weight, boundaries, span_counts,
    up_weight, up_bias, inner_gain, query_weight, key_weight, value_weight, return_weight,
):
    tile = pltpu.VMEM((8, 128), f32)
    rings = []
    for y_first in (True, False, True, False, True, False):
        rings += ring_sems(y_first)
    return pl.pallas_call(
        kernel,
        out_shape=jax.ShapeDtypeStruct((ROWS, 128), bf16),
        in_specs=[SM] + [VM] * 5 + [pl.BlockSpec(memory_space=pl.ANY)] * 9,
        out_specs=VM,
        scratch_shapes=[
            pltpu.SMEM((64,), jnp.int32),
            pltpu.VMEM((ROWS, 1024), bf16), pltpu.VMEM((1024, 128), bf16), pltpu.VMEM((1024, 128), bf16),
            pltpu.VMEM((512, 1024), bf16),
            pltpu.VMEM((ROWS, 128), f32), pltpu.VMEM((ROWS, 128), f32),
            tile, pltpu.VMEM((NZ, 8, 128), f32), tile, pltpu.VMEM((NY, 8, 128), f32),
            pltpu.VMEM((ROWS, 1024), bf16), pltpu.VMEM((1024, 1024), bf16),
            pltpu.VMEM((NY, NZ, 16, 512), bf16), pltpu.VMEM((NY, NZ, 64, 256), bf16),
            pltpu.VMEM((NY, NZ, 64, 512), bf16), pltpu.VMEM((NY, NZ, CAP, 256), bf16),
            pltpu.VMEM((2, NY, CAP, 256), bf16),
            pltpu.VMEM((ROWS, 1024), bf16), pltpu.VMEM((CAP, 4096), bf16),
            pltpu.VMEM((GROUP * CAP, CAP), f32), pltpu.VMEM((GROUP * CAP, CAP), f32),
            pltpu.VMEM((GROUP * CAP, HEAD), f32),
            pltpu.VMEM((CAP, 1024), bf16), pltpu.VMEM((8, CAP, 128), bf16),
            DMA((NZ,)), DMA((NZ,)), DMA((NY,)), DMA((NY,)),
            DMA((8,)), DMA((8,)), DMA((8,)), DMA((8,)), DMA((8,)), DMA((8,)), DMA((8,)), DMA((8,)),
            DMA((9,)),
        ] + rings,
        compiler_params=pltpu.CompilerParams(collective_id=1, has_side_effects=True, vmem_limit_bytes=58 << 20),
        name="window",
    )(
        span_counts, boundaries, outer_gain, decay_rate, up_bias, inner_gain,
        byte_states, mamba_input, mamba_step, mixer_weight,
        up_weight, query_weight, key_weight, value_weight, return_weight,
    )


def solution(mesh):
    in_specs = (
        P("seq", None), P(), P(None, "mp"), P(None, "mp"), P("mp"), P("mp", None), P("seq", None), P(),
        P("seq", "mp"), P("mp"), P(), P("seq", "mp"), P("seq", "mp"), P("seq", "mp"), P("mp", None),
    )
    return jax.shard_map(on_device, mesh=mesh, in_specs=in_specs, out_specs=P("seq", "mp"), check_vma=False)
```

```python
import math

import jax
import jax.numpy as jnp
from jax import lax
from jax.experimental import pallas as pl
from jax.experimental.pallas import tpu as pltpu
from jax.sharding import PartitionSpec as P

HEADS = 32
KV_HEADS = 8
HEAD = 128
GROUP = HEADS // KV_HEADS
NY, NZ = 4, 16
NX, NC = 4, 2
CAP = 128
ROWS = 256
KV_A = 32
Q_A = 32
STEPS = (8, 7)

eps = 1e-05
masked = -1e30
far_index = 1073741824

MESH = pl.DeviceIdType.MESH
VM = pl.BlockSpec(memory_space=pltpu.VMEM)
SM = pl.BlockSpec(memory_space=pltpu.SMEM)
DMA = pltpu.SemaphoreType.DMA
f32, bf16 = jnp.float32, jnp.bfloat16


def coords():
    s, m = lax.axis_index("seq"), lax.axis_index("mp")
    return s // NZ, s % NZ, m // NC, m % NC


def remote(src, dst, ss, rs, s, m):
    return pltpu.make_async_remote_copy(
        src_ref=src, dst_ref=dst, send_sem=ss, recv_sem=rs, device_id=(s, m), device_id_type=MESH
    )


def when(cond, f):
    if isinstance(cond, bool):
        if cond:
            f()
    else:
        pl.when(cond)(f)


def loop(lo, hi, f):
    def body(i, _):
        f(i)
        return 0

    lax.fori_loop(lo, hi, body, 0)


class PushY:
    def __init__(self, buf, lo, hi, ss, rs, place, causal=False):
        self.buf, self.lo, self.n, self.ss, self.rs, self.causal = buf, lo, hi - lo, ss, rs, causal
        self.y, self.z, self.m = place

    def to(self, k):
        return self.y + k < NY if self.causal else True

    def of(self, k):
        return self.y >= k if self.causal else True

    def copy(self, k, yy, zz, slot):
        ref = self.buf.at[yy % NY, zz, pl.ds(self.lo, self.n)]
        return remote(ref, ref, self.ss.at[0], self.rs.at[slot], (self.y + k) % NY * NZ + self.z, self.m)

    def start(self, zz, slot):
        for k in (2, 1, 3):
            when(self.to(k), lambda: self.copy(k, self.y, zz, k if slot is None else slot).start())

    def came(self, k):
        self.copy(k, self.y + NY - k, self.z, k).wait_recv()

    def wait(self, columns, slot=0):
        if self.causal:
            pl.when(self.y > 0)(lambda: self.take(self.rs.at[slot], columns))
            return
        ref = self.buf.at[pl.ds(0, 3), pl.ds(0, columns), pl.ds(self.lo, self.n)]
        pltpu.make_async_copy(ref, ref, self.rs.at[slot]).wait()

    def take(self, sem, columns, sent=False):
        for n in range(1, NY):
            ref = self.buf.at[pl.ds(0, n), pl.ds(0, columns), pl.ds(self.lo, self.n)]
            have = self.y == (NY - 1 - n if sent else n)
            pl.when(have)(lambda: pltpu.make_async_copy(ref, ref, sem).wait())

    def drain(self, columns):
        if self.causal:
            self.take(self.ss.at[0], columns, True)
            return
        ref = self.buf.at[pl.ds(0, 3), pl.ds(0, columns), pl.ds(self.lo, self.n)]
        pltpu.make_async_copy(ref, ref, self.ss.at[0]).wait()


class RingZ:
    def __init__(self, buf, lo, hi, k, ss, rs, place):
        self.buf, self.lo, self.n, self.k, self.ss, self.rs = buf, lo, hi - lo, k, ss, rs
        self.y, self.z, self.m = place

    def item(self, d, t):
        return (self.z + (NZ - t if d == 0 else t)) % NZ

    def copy(self, d, t, zz):
        ref = self.buf.at[(self.y + self.k) % NY, zz, pl.ds(self.lo, self.n)]
        to = (self.z + (1 if d == 0 else NZ - 1)) % NZ
        return remote(ref, ref, self.ss.at[0], self.rs.at[2 * self.k + d, t], self.y * NZ + to, self.m)

    def own(self):
        for d in range(2):
            self.copy(d, 0, self.z).start()

    def step(self, d, t):
        zz = self.item(d, t)
        self.copy(d, t - 1, zz).wait_recv()
        when(t < STEPS[d], lambda: self.copy(d, t, zz).start())

    def drain(self, blocks):
        ref = self.buf.at[pl.ds(0, blocks), pl.ds(0, NZ - 1), pl.ds(self.lo, self.n)]
        pltpu.make_async_copy(ref, ref, self.ss.at[0]).wait()


class YFirst:
    def __init__(self, buf, lo, hi, sems, place, causal=False):
        yss, yrs, zss, zrs = sems
        self.y, self.z, self.causal = place[0], place[1], causal
        self.push = PushY(buf, lo, hi, yss, yrs, place, causal)
        self.rings = [RingZ(buf, lo, hi, k, zss, zrs, place) for k in range(NY)]

    def own(self):
        self.push.start(self.z, None)
        self.rings[0].own()

    def spread(self):
        for k in (1, 3, 2):
            def go():
                self.push.came(k)
                self.rings[NY - k].own()
            when(self.push.of(k), go)

    def step(self, t):
        for d in range(2):
            def go():
                for k in (0, 3, 1, 2):
                    when(self.push.of(NY - k) if k else True, lambda: self.rings[k].step(d, t))
            when(t <= STEPS[d], go)

    def drain(self):
        self.push.drain(1)
        if self.causal:
            for n in range(1, NY + 1):
                pl.when(self.y == n - 1)(lambda: self.rings[0].drain(n))
        else:
            self.rings[0].drain(NY)


class ZFirst:
    def __init__(self, buf, lo, hi, sems, place, by_column=False):
        yss, yrs, zss, zrs = sems
        self.z, self.by_column = place[1], by_column
        self.push = PushY(buf, lo, hi, yss, yrs, place, by_column)
        self.ring = RingZ(buf, lo, hi, 0, zss, zrs, place)

    def start(self, zz):
        self.push.start(zz, zz if self.by_column else 0)

    def own(self):
        self.ring.own()
        self.start(self.z)

    def step(self, t):
        for d in range(2):
            def go():
                self.ring.step(d, t)
                self.start(self.ring.item(d, t))
            when(t <= STEPS[d], go)

    def finish(self):
        self.push.wait(NZ)

    def drain(self):
        self.push.drain(NZ)
        self.ring.drain(1)


def ring_sems(y_first):
    zs = (8, 8) if y_first else (2, 8)
    return [DMA((1,)), DMA((NZ,)), DMA((1,)), DMA(zs)]


class MpGather:
    def __init__(self, view, ss, rs, place):
        self.view, self.ss, self.rs = view, ss, rs
        self.s, self.x, self.c = place

    def same(self, k, back):
        ref = self.view(((self.x + (NX - k if back else 0)) % NX) * NC + self.c)
        return remote(ref, ref, self.ss.at[k], self.rs.at[k], self.s, ((self.x + k) % NX) * NC + self.c)

    def across(self, k, core):
        ref = self.view(((self.x + NX - k) % NX) * NC + core)
        return remote(ref, ref, self.ss.at[4 + k], self.rs.at[4 + k], self.s, self.x * NC + 1 - self.c)

    def start(self):
        for k in (2, 1, 3):
            self.same(k, False).start()
        self.across(0, self.c).start()

    def relay(self):
        for k in (1, 3, 2):
            self.same(k, True).wait_recv()
            self.across(k, self.c).start()

    def finish(self):
        for k in (0, 1, 3, 2):
            self.across(k, 1 - self.c).wait_recv()

    def drain(self):
        for k in (1, 2, 3):
            self.same(k, False).wait_send()
        for k in range(4):
            self.across(k, self.c).wait_send()


def one_minus_exp(v):
    series = v * (1.0 - v * (0.5 - v * (1 / 6 - v * (1 / 24 - v * (1 / 120 - v / 720)))))
    return jnp.where(v < 0.25, series, 1.0 - jnp.exp(-v))


def scan_rows(decays, drives):
    rows = decays.shape[0]
    ids = lax.broadcasted_iota(jnp.int32, decays.shape, 0)
    k = 1
    while k < rows:
        if k < 8:
            a_back = jnp.where(ids >= k, pltpu.roll(decays, k, 0), 1.0)
            b_back = jnp.where(ids >= k, pltpu.roll(drives, k, 0), 0.0)
        else:
            a_back = jnp.concatenate([jnp.ones((k, decays.shape[1]), f32), decays[: rows - k]], 0)
            b_back = jnp.concatenate([jnp.zeros((k, decays.shape[1]), f32), drives[: rows - k]], 0)
        drives = decays * b_back + drives
        decays = decays * a_back
        k *= 2
    return decays, drives


def block_cols(m, width=128):
    return pl.ds(pl.multiple_of(m * width, 128), width)


def row_of(ref):
    return ref[...].reshape(1, ref.shape[0])


def kernel(
    counts_ref, marks_ref, gain_ref, rate_ref, bias_ref, igain_ref,
    bytes_hbm, win_hbm, wstep_hbm, mixer_hbm, up_hbm, wq_hbm, wk_hbm, wv_hbm, wret_hbm,
    out_ref,
    offs_ref, bytes_ref, win_ref, wstep_ref, wret_ref, through_ref, local_ref, pair_ref, line_ref, total_ref, col_ref,
    states_ref, mix_ref, u_ref, kvw_ref, q_ref, kv_ref, stage_ref, enc_ref, wide_ref, peak_ref, denom_ref, acc_ref,
    part_ref, box_ref,
    pzs, pzr, pys, pyr, gs, gr, ms, mr, ws, wr, bs, br, lsem, *ring,
):
    y, z, x, c = coords()
    s, m = y * NZ + z, x * NC + c
    place = (y, z, m)
    peers = [(y * NZ + (z + k) % NZ, m) for k in range(1, NZ)]
    peers += [((y + k) % NY * NZ + z, m) for k in range(1, NY)]
    peers += [(s, (m + k) % 8) for k in range(1, 8)]
    barrier = pltpu.get_barrier_semaphore()
    for seq, mp in peers:
        pl.semaphore_signal(barrier, inc=1, device_id=(seq, mp), device_id_type=MESH)

    u = YFirst(u_ref, 0, 16, ring[0:4], place)
    kvw = ZFirst(kvw_ref, 0, 64, ring[4:8], place)
    qa = YFirst(q_ref, 0, Q_A, ring[8:12], place)
    qb = ZFirst(q_ref, Q_A, 64, ring[12:16], place)
    kva = YFirst(kv_ref, 0, KV_A, ring[16:20], place, causal=True)
    kvb = ZFirst(kv_ref, KV_A, CAP, ring[20:24], place, by_column=True)
    mixer = MpGather(lambda mm: mix_ref.at[pl.ds(pl.multiple_of(mm * 128, 128), 128)], ms, mr, (s, x, c))
    g = MpGather(lambda mm: states_ref.at[:, block_cols(mm)], gs, gr, (s, x, c))
    w = MpGather(lambda mm: wide_ref.at[:, block_cols(mm, 512)], ws, wr, (s, x, c))

    copies = [
        pltpu.make_async_copy(src, dst, lsem.at[i])
        for i, (src, dst) in enumerate([
            (bytes_hbm, bytes_ref),
            (win_hbm, win_ref),
            (wstep_hbm, wstep_ref),
            (up_hbm, u_ref.at[y, z]),
            (wk_hbm, kvw_ref.at[y, z, :, pl.ds(0, HEAD)]),
            (wv_hbm, kvw_ref.at[y, z, :, pl.ds(HEAD, HEAD)]),
            (wq_hbm, q_ref.at[y, z]),
            (mixer_hbm, mixer.view(m)),
            (wret_hbm, wret_ref),
        ])
    ]
    for cp in copies:
        cp.start()

    def offsets(i, acc):
        offs_ref[i] = acc
        return acc + counts_ref[i]

    lax.fori_loop(0, 64, offsets, jnp.int32(0))
    for cp in copies[:3]:
        cp.wait()

    values = bytes_ref[...].astype(f32)
    scale = lax.rsqrt(jnp.mean(values * values, axis=-1, keepdims=True) + eps)
    normed = (values * scale * row_of(gain_ref)).astype(bf16)
    inputs = jnp.dot(normed, win_ref[...], preferred_element_type=f32)
    raw = jnp.dot(normed, wstep_ref[...], preferred_element_type=f32)
    rate = (jnp.maximum(raw, 0.0) + jnp.log1p(jnp.exp(-jnp.abs(raw)))) * row_of(rate_ref)
    through, local = scan_rows(jnp.exp(-rate), jnp.sqrt(one_minus_exp(2.0 * rate)) * inputs)
    through_ref[...] = through
    local_ref[...] = local
    tile = jnp.concatenate([through[ROWS - 1 :], local[ROWS - 1 :], jnp.zeros((6, 128), f32)], 0)
    pair_ref[...] = tile
    line_ref[z] = tile
    for cp in copies[3:]:
        cp.wait()

    def clear(yy):
        kv_ref[yy] = jnp.zeros((NZ, CAP, 2 * HEAD), bf16)

    loop(y + 1, NY, clear)
    pl.semaphore_wait(barrier, len(peers))

    def zpush(k):
        return remote(pair_ref, line_ref.at[z], pzs.at[k], pzr.at[k], y * NZ + (z + k) % NZ, m)

    def zcame(k):
        ref = line_ref.at[(z + NZ - k) % NZ]
        return remote(ref, ref, pzs.at[k], pzr.at[k], y * NZ + (z + k) % NZ, m)

    def ypush(k):
        return remote(total_ref, col_ref.at[y], pys.at[k], pyr.at[k], (y + k) % NY * NZ + z, m)

    def ycame(k):
        ref = col_ref.at[(y + NY - k) % NY]
        return remote(ref, ref, pys.at[k], pyr.at[k], (y + k) % NY * NZ + z, m)

    def step_a(t):
        u.step(t)
        kvw.step(t)

    def step_q(t):
        qa.step(t)
        qb.step(t)

    loop(1, NZ, lambda k: zpush(k).start())
    u.own()
    kvw.own()
    qa.own()
    qb.own()
    mixer.start()
    u.spread()
    qa.spread()
    step_a(1)
    loop(1, NZ, lambda k: zcame(k).wait_recv())
    zero, one = jnp.zeros((1, 128), f32), jnp.ones((1, 128), f32)

    def fold(zz, carry):
        pair = line_ref[zz]
        return carry[0] * pair[0:1], pair[0:1] * carry[1] + pair[1:2]

    before = lax.fori_loop(0, z, fold, (one, zero))
    whole = lax.fori_loop(z, NZ, fold, before)
    tile = jnp.concatenate([whole[0], whole[1], jnp.zeros((6, 128), f32)], 0)
    total_ref[...] = tile
    col_ref[y] = tile
    for k in range(1, NY):
        ypush(k).start()
    step_a(2)
    step_q(1)
    for k in range(1, NY):
        ycame(k).wait_recv()

    def fold_y(yy, h):
        pair = col_ref[yy]
        return pair[0:1] * h + pair[1:2]

    arriving = before[0] * lax.fori_loop(0, y, fold_y, zero) + before[1]
    states_ref[:, block_cols(m)] = (local_ref[...] + through_ref[...] * arriving).astype(bf16)
    g.start()
    mixer.relay()
    step_a(3)
    step_q(2)
    g.relay()
    step_a(4)
    g.finish()
    mixer.finish()
    step_q(3)

    mixed = jnp.dot(states_ref[...], mix_ref[...], preferred_element_type=f32)
    enc_ref[...] = (bytes_ref[...].astype(f32) + mixed).astype(bf16)
    step_a(5)
    marks = marks_ref[...]
    byte_ids = lax.broadcasted_iota(jnp.int32, (ROWS, CAP), 0)
    pick = jnp.where(jnp.minimum(marks, ROWS - 1) == byte_ids, 1.0, 0.0).astype(bf16)
    pooled = lax.dot_general(
        pick, enc_ref[...], (((0,), (0,)), ((), ())), preferred_element_type=f32
    ).astype(bf16)
    step_a(6)
    step_q(4)
    loop(7, 9, step_a)
    u_full = u_ref[...].reshape(1024, 512)
    share = jnp.dot(pooled, u_full, preferred_element_type=f32) + row_of(bias_ref)
    wide_ref[:, block_cols(m, 512)] = share.astype(bf16)
    w.start()
    loop(5, 7, step_q)
    w.relay()
    step_q(7)
    w.finish()
    wide = wide_ref[...].astype(f32)
    scale = lax.rsqrt(jnp.mean(wide * wide, axis=-1, keepdims=True) + eps)
    wide_n = (wide * scale * row_of(igain_ref)).astype(bf16)
    kvw.finish()
    kv = jnp.dot(wide_n, kvw_ref[...].reshape(4096, 256), preferred_element_type=f32)
    kv_ref[y, z] = kv.astype(bf16)
    kva.own()
    kvb.own()
    kva.spread()

    def step_kv(t):
        kva.step(t)
        kvb.step(t)

    step_q(8)
    loop(1, 3, step_kv)
    qb.finish()
    queries = jnp.dot(wide_n, q_ref[...].reshape(4096, 512), preferred_element_type=f32).astype(bf16)
    stacked = jnp.concatenate([queries[:, h * HEAD : (h + 1) * HEAD] for h in range(GROUP)], 0)

    total = GROUP * CAP
    own_rows = offs_ref[s] + (lax.broadcasted_iota(jnp.int32, (total, 1), 0) & (CAP - 1))
    slots = lax.broadcasted_iota(jnp.int32, (1, CAP), 1)
    peak_ref[...] = jnp.full((total, CAP), masked, f32)
    denom_ref[...] = jnp.zeros((total, CAP), f32)
    acc_ref[...] = jnp.zeros((total, HEAD), f32)

    def ids_of(zz):
        return [
            jnp.where(slots < counts_ref[yy * NZ + zz], offs_ref[yy * NZ + zz] + slots, far_index)
            for yy in range(NY)
        ]

    def turn(j):
        pl.when(j <= 5)(lambda: step_kv(j + 3))
        columns = ((z + j) % NZ, (z + NZ - 1 - j) % NZ)
        staged = []
        for i, zz in enumerate(columns):
            kvb.push.wait(1, zz)
            staged.append(pltpu.make_async_copy(kv_ref.at[:, zz], stage_ref.at[i], lsem.at[i]))
            staged[i].start()
        ids = jnp.concatenate(ids_of(columns[0]) + ids_of(columns[1]), 1)
        for cp in staged:
            cp.wait()
        kv = stage_ref[...].reshape(2 * NY * CAP, 2 * HEAD)
        scores = lax.dot_general(stacked, kv[:, :HEAD], (((1,), (1,)), ((), ())), preferred_element_type=f32)
        scores = jnp.where(ids <= own_rows, scores * (1.0 / math.sqrt(HEAD)), masked)
        peak = peak_ref[:, 0:1]
        new_peak = jnp.maximum(peak, jnp.max(scores, axis=1, keepdims=True))
        shrink = jnp.exp(peak - new_peak)
        lifted = jnp.exp(scores - new_peak)
        denom = denom_ref[:, 0:1] * shrink + jnp.sum(lifted, axis=1, keepdims=True)
        acc = jnp.dot(lifted.astype(bf16), kv[:, HEAD:], preferred_element_type=f32)
        acc_ref[...] = acc_ref[...] * shrink + acc
        peak_ref[...] = jnp.broadcast_to(new_peak, (total, CAP))
        denom_ref[...] = jnp.broadcast_to(denom, (total, CAP))

    loop(0, 8, turn)
    attended = (acc_ref[...] / denom_ref[...]).astype(bf16)
    attended = jnp.concatenate([attended[h * CAP : (h + 1) * CAP] for h in range(GROUP)], 1)

    part_ref[...] = jnp.dot(attended, wret_ref[...], preferred_element_type=f32).astype(bf16)

    def push(k):
        to = (m + k) % 8
        return remote(part_ref.at[:, block_cols(to)], box_ref.at[k], bs.at[k], br.at[k], s, to)

    for k in range(1, 8):
        push(k).start()
    live = (marks <= byte_ids) & (lax.broadcasted_iota(jnp.int32, (ROWS, CAP), 1) < counts_ref[s])
    passed = jnp.sum(jnp.where(live, 1.0, 0.0), axis=1, keepdims=True)
    lane = lax.broadcasted_iota(jnp.int32, (ROWS, CAP), 1).astype(f32)
    spread = jnp.where(passed - 1.0 == lane, 1.0, 0.0).astype(bf16)

    for gather in (mixer, g, w):
        gather.drain()
    loop(1, NZ, lambda k: zpush(k).wait_send())
    for k in range(1, NY):
        ypush(k).wait_send()
    for stream in (u, kvw, qa, qb, kva, kvb):
        stream.drain()

    acc = part_ref[:, block_cols(m)].astype(f32)
    for k in range(1, 8):
        push(k).wait_recv()
        acc = acc + box_ref[k].astype(f32)
    back = jnp.dot(spread, acc.astype(bf16), preferred_element_type=f32)
    out_ref[...] = (enc_ref[:, block_cols(m)].astype(f32) + back).astype(bf16)
    for k in range(1, 8):
        push(k).wait_send()


def on_device(
    byte_states, outer_gain, mamba_input, mamba_step, decay_rate, mixer_weight, boundaries, span_counts,
    up_weight, up_bias, inner_gain, query_weight, key_weight, value_weight, return_weight,
):
    tile = pltpu.VMEM((8, 128), f32)
    rings = []
    for y_first in (True, False, True, False, True, False):
        rings += ring_sems(y_first)
    return pl.pallas_call(
        kernel,
        out_shape=jax.ShapeDtypeStruct((ROWS, 128), bf16),
        in_specs=[SM] + [VM] * 5 + [pl.BlockSpec(memory_space=pl.ANY)] * 9,
        out_specs=VM,
        scratch_shapes=[
            pltpu.SMEM((64,), jnp.int32),
            pltpu.VMEM((ROWS, 1024), bf16), pltpu.VMEM((1024, 128), bf16), pltpu.VMEM((1024, 128), bf16),
            pltpu.VMEM((512, 1024), bf16),
            pltpu.VMEM((ROWS, 128), f32), pltpu.VMEM((ROWS, 128), f32),
            tile, pltpu.VMEM((NZ, 8, 128), f32), tile, pltpu.VMEM((NY, 8, 128), f32),
            pltpu.VMEM((ROWS, 1024), bf16), pltpu.VMEM((1024, 1024), bf16),
            pltpu.VMEM((NY, NZ, 16, 512), bf16), pltpu.VMEM((NY, NZ, 64, 256), bf16),
            pltpu.VMEM((NY, NZ, 64, 512), bf16), pltpu.VMEM((NY, NZ, CAP, 256), bf16),
            pltpu.VMEM((2, NY, CAP, 256), bf16),
            pltpu.VMEM((ROWS, 1024), bf16), pltpu.VMEM((CAP, 4096), bf16),
            pltpu.VMEM((GROUP * CAP, CAP), f32), pltpu.VMEM((GROUP * CAP, CAP), f32),
            pltpu.VMEM((GROUP * CAP, HEAD), f32),
            pltpu.VMEM((CAP, 1024), bf16), pltpu.VMEM((8, CAP, 128), bf16),
            DMA((NZ,)), DMA((NZ,)), DMA((NY,)), DMA((NY,)),
            DMA((8,)), DMA((8,)), DMA((8,)), DMA((8,)), DMA((8,)), DMA((8,)), DMA((8,)), DMA((8,)),
            DMA((9,)),
        ] + rings,
        compiler_params=pltpu.CompilerParams(collective_id=1, has_side_effects=True, vmem_limit_bytes=58 << 20),
        name="window",
    )(
        span_counts, boundaries, outer_gain, decay_rate, up_bias, inner_gain,
        byte_states, mamba_input, mamba_step, mixer_weight,
        up_weight, query_weight, key_weight, value_weight, return_weight,
    )


def solution(mesh):
    in_specs = (
        P("seq", None), P(), P(None, "mp"), P(None, "mp"), P("mp"), P("mp", None), P("seq", None), P(),
        P("seq", "mp"), P("mp"), P(), P("seq", "mp"), P("seq", "mp"), P("seq", "mp"), P("mp", None),
    )
    return jax.shard_map(on_device, mesh=mesh, in_specs=in_specs, out_specs=P("seq", "mp"), check_vma=False)
```
